128 devices in a mesh: seq: 32 (over z, y, core), head: 4 (over x).
Axes of the slice: x: 4, y: 4, z: 4, core: 2. Of those that a mesh axis runs over, the one named last changes fastest.
Arguments:
- tokens: bfloat16 [98304, 768], P('seq'), may hold values from -6 to 6
- w_query: bfloat16 [768, 768], P(None, 'head'), may hold values from -0.21875 to 0.21875
- w_key: bfloat16 [768, 768], P(None, 'head'), may hold values from -0.21875 to 0.21875
- w_value: bfloat16 [768, 768], P(None, 'head'), may hold values from -0.21875 to 0.21875
- freq: float32 [64, 128], replicated, may hold values from -1.5 to 1.5
- w_out: bfloat16 [768, 768], replicated, may hold values from -0.21875 to 0.21875
- router: bfloat16 [768, 128], replicated, may hold values from -0.21875 to 0.21875
- w_in: bfloat16 [128, 768, 3072], P(('seq', 'head')), may hold values from -0.21875 to 0.21875
- w_down: bfloat16 [128, 3072, 768], P(('seq', 'head')), may hold values from -0.109375 to 0.109375
- picks: int32 [128, 128, 6], P(None, ('seq', 'head')), may hold values from 0 to 767, as said below
Outputs:
- layer_out: bfloat16 [98304, 768], P(('seq', 'head'))
The draws below stay inside these ranges and needn't reach their ends.
Inputs may be any that keep to these rules, and one draw needn't show every extreme that they name: `picks`: for each expert and each source block the 6 picked rows are distinct.
All inputs are finite; a program needn't handle non-finite values.
Results may differ from the reference program's by a relative error of at most 0.017.
Values may be sent and summed in bfloat16 or wider, within the bound.
A program may use at most 128 MiB of HBM per device.

```python
import math
import jax
import jax.numpy as jnp
from jax import lax

D = 768
HEADS = 12
HD = 64
FEAT = 256
FF = 3072
BLOCK = 512
CAP = 6
TOKENS = 98304
EXPERTS = 128
ROWS = 768


def draw_picks(key, part):
    scores = jax.random.randint(key, (EXPERTS, EXPERTS, ROWS), 0, 4096)
    row_ids = jnp.arange(ROWS, dtype=jnp.int32)[None, None, :]
    expert_ids = jnp.arange(EXPERTS, dtype=jnp.int32)[:, None, None]
    first = (expert_ids == 0) & (row_ids == 0)
    last = (expert_ids == 0) & (row_ids == ROWS - 1)
    scores = jnp.where(first, -2, jnp.where(last, -1, scores))
    order = jnp.argsort(scores * ROWS + row_ids, axis=-1, stable=True)
    return order[..., :CAP].astype(jnp.int32)


def block_levels(rng, dims, pieces, smallest, top_value):
    def one(axis_at, blocks):
        steps = jax.random.uniform(jax.random.fold_in(jax.random.fold_in(rng, 6), axis_at), (blocks,), jnp.float32, smallest / len(pieces), top_value / len(pieces))
        return jnp.repeat(jnp.exp(steps), dims[axis_at] // blocks).reshape((-1,) + (1,) * (len(dims) - axis_at - 1))

    factor_of = one(*pieces[0])
    for cut in pieces[1:]:
        factor_of = factor_of * one(*cut)
    return factor_of


def bell_draw(key, extent, deviation, most, cuts=(), kind=jnp.bfloat16):
    array = jax.random.normal(key, extent, jnp.float32) * deviation
    if len(cuts) > 0:
        array = block_levels(key, extent, cuts, -0.22, 0.18) * array
    return jnp.clip(array, min=-most, max=most).astype(kind)


def setup_inputs(seed: int = 0) -> dict:
    key_of = jax.random.split(jax.random.key(seed), 11)
    tokens = bell_draw(key_of[0], (TOKENS, D), 1.0, 6.0, ((0, 32),))
    w_query = bell_draw(key_of[1], (D, D), D ** -0.5, 0.21875, ((1, 4),))
    w_key = bell_draw(key_of[2], (D, D), D ** -0.5, 0.21875, ((1, 4),))
    w_value = bell_draw(key_of[3], (D, D), D ** -0.5, 0.21875, ((1, 4),))
    freq = bell_draw(key_of[4], (HD, FEAT // 2), 0.25, 1.5, (), jnp.float32)
    w_out = bell_draw(key_of[5], (D, D), D ** -0.5, 0.21875)
    router = bell_draw(key_of[6], (D, EXPERTS), D ** -0.5, 0.21875)
    w_in = bell_draw(key_of[7], (EXPERTS, D, FF), D ** -0.5, 0.21875, ((0, 128),))
    w_down = bell_draw(key_of[8], (EXPERTS, FF, D), FF ** -0.5, 0.109375, ((0, 128),))
    picks = draw_picks(jax.random.fold_in(key_of[10], 71), 0)
    return dict(tokens=tokens, w_query=w_query, w_key=w_key, w_value=w_value, freq=freq, w_out=w_out, router=router, w_in=w_in, w_down=w_down, picks=picks)


EPS = 1e-06

def features(projected, freq, heads):
    rows = projected.shape[0]
    split = projected.reshape(rows, heads, -1).astype(jnp.float32)
    phase = jnp.einsum('thd,df->thf', split, freq, precision=lax.Precision.HIGHEST)
    scale = 1.0 / math.sqrt(freq.shape[1])
    return (jnp.concatenate([jnp.cos(phase), jnp.sin(phase)], axis=-1) * scale).astype(jnp.bfloat16)

def local_pass(qf, kf, vals, block, start_state):
    total, heads, feat = qf.shape
    width = vals.shape[2]
    count = total // block
    q_blocks = qf.reshape(count, block, heads, feat)
    k_blocks = kf.reshape(count, block, heads, feat)
    v_blocks = vals.reshape(count, block, heads, width)
    causal = jnp.arange(block)[:, None] >= jnp.arange(block)[None, :]

    def advance(state, blocks):
        q_part, k_part, v_part = blocks
        scores = jnp.einsum('bhf,chf->hbc', q_part.astype(jnp.float32), k_part.astype(jnp.float32))
        scores = jnp.where(causal[None], scores, 0.0).astype(jnp.bfloat16)
        inner = jnp.einsum('hbc,chd->bhd', scores.astype(jnp.float32), v_part.astype(jnp.float32))
        carried = jnp.einsum('bhf,hfd->bhd', q_part.astype(jnp.float32), state, precision=lax.Precision.HIGHEST)
        state = state + jnp.einsum('chf,chd->hfd', k_part.astype(jnp.float32), v_part.astype(jnp.float32))
        return (state, inner + carried)
    final, outs = lax.scan(advance, start_state, (q_blocks, k_blocks, v_blocks))
    return outs.reshape(total, heads, width)

def reference(tokens, w_query, w_key, w_value, freq, w_out, router, w_in, w_down, picks):
    query = jnp.dot(tokens, w_query, preferred_element_type=jnp.float32).astype(jnp.bfloat16)
    key = jnp.dot(tokens, w_key, preferred_element_type=jnp.float32).astype(jnp.bfloat16)
    value = jnp.dot(tokens, w_value, preferred_element_type=jnp.float32).astype(jnp.bfloat16)
    q_feat = features(query, freq, HEADS)
    k_feat = features(key, freq, HEADS)
    vals = value.reshape(TOKENS, HEADS, HD)
    start_state = jnp.zeros((HEADS, FEAT, HD), jnp.float32)
    raw = local_pass(q_feat, k_feat, vals, BLOCK, start_state)
    meansq = lax.optimization_barrier(jnp.mean(raw * raw, axis=-1, keepdims=True))
    attn = (raw * lax.rsqrt(meansq + EPS)).astype(jnp.bfloat16).reshape(TOKENS, D)
    hidden_state = (tokens.astype(jnp.float32) + jnp.dot(attn, w_out, preferred_element_type=jnp.float32)).astype(jnp.bfloat16)
    gate = jax.nn.sigmoid(jnp.dot(hidden_state, router, preferred_element_type=jnp.float32)).astype(jnp.bfloat16)
    block_rows = TOKENS // EXPERTS
    places = (jnp.arange(EXPERTS, dtype=jnp.int32)[None, :, None] * block_rows + picks).astype(jnp.int32)
    flat = places.reshape(EXPERTS, -1)

    def expert(inputs):
        place, first, second = inputs
        chosen = hidden_state[place]
        inner = jax.nn.gelu(jnp.dot(chosen, first, preferred_element_type=jnp.float32), approximate=True).astype(jnp.bfloat16)
        return jnp.dot(inner, second, preferred_element_type=jnp.float32).astype(jnp.bfloat16)
    expert_out = lax.map(expert, (flat, w_in, w_down))
    weight = gate[flat, jnp.arange(EXPERTS, dtype=jnp.int32)[:, None]]
    contrib = weight.astype(jnp.float32)[..., None] * expert_out.astype(jnp.float32)
    moe = jnp.zeros((TOKENS, D), jnp.float32).at[flat.reshape(-1)].add(contrib.reshape(-1, D))
    return (hidden_state.astype(jnp.float32) + moe).astype(jnp.bfloat16)
```

```python
import functools
import math

import jax
import jax.numpy as jnp
from jax import lax
from jax.experimental import pallas as pl
from jax.experimental.pallas import tpu as pltpu
from jax.sharding import Mesh
from jax.sharding import PartitionSpec as P

MESH = pl.DeviceIdType.MESH
AXES = ("z", "y", "c", "head")
HD = 64
CHUNK = 256
EPS = 1e-06
F32 = jnp.float32
BF16 = jnp.bfloat16

SCALE = 1.0 / math.sqrt(128.0)
ROOT = math.sqrt(2.0 * SCALE)
SIN = [ROOT * v for v in (3.141582022210377, -5.167142797933202, 2.541899038850396, -0.5546362211874226)]
COS = [
    ROOT * v
    for v in (
        0.9999999535200743,
        -4.93479286153638,
        4.0584119554710245,
        -1.3318803818997542,
        0.21969719133234294,
    )
]
ROUNDER = 12582912.0


def nt(a, b):
    return lax.dot_general(a, b, (((1,), (1,)), ((), ())), preferred_element_type=F32)


def nn(a, b):
    return lax.dot_general(a, b, (((1,), (0,)), ((), ())), preferred_element_type=F32)


def tn(a, b):
    return lax.dot_general(a, b, (((0,), (0,)), ((), ())), preferred_element_type=F32)


def waves(turns):
    r = turns - ((turns + ROUNDER) - ROUNDER)
    y = r * r
    a = r * (SIN[0] + y * (SIN[1] + y * (SIN[2] + y * SIN[3])))
    b = COS[0] + y * (COS[1] + y * (COS[2] + y * (COS[3] + y * COS[4])))
    return (SCALE - a * a).astype(BF16), (a * b).astype(BF16)


def feature_heads(x, wx, wf01, wf2):
    proj = nn(x, wx).astype(BF16)
    pair, last = proj[:, :128], proj[:, 128:]
    cos01, sin01 = waves(nn(jnp.concatenate([pair, pair], axis=1), wf01))
    cos2, sin2 = waves(nn(last, wf2))
    return (
        jnp.concatenate([cos01[:, :128], sin01[:, :128]], axis=1),
        jnp.concatenate([cos01[:, 128:], sin01[:, 128:]], axis=1),
        jnp.concatenate([cos2, sin2], axis=1),
    )


def attention_kernel(
    tok, wq, wk, wv, freq, out,
    xbuf, wqx, wkx, wvt, wf01, wf2, kf, qf, vt, before, intra, run, prefix,
    cs, cr, ys, yr, zs, zr, fs, fr, att,
    xsem, csem, ysend, yrecv, zsend, zrecv, hsend, hrecv,
):
    z, y, c, x = (lax.axis_index(a) for a in AXES)
    heads = 3
    chunks = xbuf.shape[0]
    per = chunks // 4

    def fetch(i):
        return pltpu.make_async_copy(
            tok.at[pl.ds(pl.multiple_of(i * CHUNK, CHUNK), CHUNK), :], xbuf.at[i], xsem.at[i]
        )

    @pl.loop(0, chunks)
    def _(i):
        fetch(i).start()

    core = (z, y, 1 - c, x)
    y_peers = [(z, y ^ k, c, x) for k in (1, 2, 3)]
    z_peers = [(z ^ k, y, c, x) for k in (1, 2, 3)]
    x_peers = [(z, y, c, x ^ k) for k in (1, 2, 3)]
    barrier = pltpu.get_barrier_semaphore()
    for peer in [core] + y_peers + z_peers + x_peers:
        pl.semaphore_signal(barrier, inc=1, device_id=peer, device_id_type=MESH)

    for src, dst in ((wq, wqx), (wk, wkx)):
        w = src[...]
        dst[:, :192] = w
        dst[:, 192:] = w[:, 128:192]
    wvt[...] = wv[...].T
    turns = freq[...] * (1.0 / (2.0 * math.pi))
    high = turns.astype(BF16)
    low = (turns - high.astype(F32)).astype(BF16)
    wf01[...] = jnp.zeros_like(wf01)
    wf01[0:64, 0:128] = high
    wf01[64:128, 128:256] = high
    wf01[128:192, 0:128] = low
    wf01[192:256, 128:256] = low
    wf2[0:64, :] = high
    wf2[64:128, :] = low
    run[...] = jnp.zeros_like(run)

    @pl.loop(0, chunks)
    def _(i):
        fetch(i).wait()
        xs = xbuf[i]
        vals = nt(wvt[...], xs).astype(BF16)
        vt[i] = vals
        feats = feature_heads(xs, wkx[...], wf01[...], wf2[...])
        before[i] = run[...]
        for h in range(heads):
            kf[h, i] = feats[h]
            run[h * HD : (h + 1) * HD, :] += nn(vals[h * HD : (h + 1) * HD, :], feats[h])

    def send(src, dst, ssem, rsem, peer):
        return pltpu.make_async_remote_copy(
            src_ref=src, dst_ref=dst, send_sem=ssem, recv_sem=rsem, device_id=peer, device_id_type=MESH
        )

    half = cs.shape[0] // 2
    mine = pl.ds(pl.multiple_of(c * half, half), half)
    other = pl.ds(pl.multiple_of((1 - c) * half, half), half)
    c_copy = send(cs, cr, csem.at[0], csem.at[1], core)
    y_copies = [send(ys, yr.at[y], ysend.at[k], yrecv.at[k], y_peers[k]) for k in range(3)]
    z_copies = [send(zs, zr.at[z], zsend.at[k], zrecv.at[k], z_peers[k]) for k in range(3)]
    f_copy = send(fs, fr, csem.at[2], csem.at[3], core)

    pl.semaphore_wait(barrier, 10)
    cs[...] = run[...].astype(BF16)
    c_copy.start()

    def scan_pieces(pieces, index):
        inside = jnp.zeros(pieces.shape[1:], F32)
        total = jnp.zeros(pieces.shape[1:], F32)
        for k in range(4):
            piece = pieces[k].astype(F32)
            inside = inside + jnp.where(k < index, piece, 0.0)
            total = total + piece
        return inside, total

    rows = lax.broadcasted_iota(jnp.int32, (CHUNK, CHUNK), 0)
    columns = lax.broadcasted_iota(jnp.int32, (CHUNK, CHUNK), 1)
    causal = rows <= columns

    @pl.loop(0, chunks)
    def _(i):
        @pl.when(i == 2)
        def _():
            c_copy.wait()
            ys[...] = (run[mine, :] + cr[mine, :].astype(F32)).astype(BF16)
            yr[y] = ys[...]
            for copy in y_copies:
                copy.start()

        @pl.when(i == 5)
        def _():
            for copy in y_copies:
                copy.wait()
            inside, total = scan_pieces(yr, y)
            prefix[mine, :] = inside
            zs[...] = total.astype(BF16)
            zr[z] = zs[...]
            for copy in z_copies:
                copy.start()

        @pl.when(i == 9)
        def _():
            for copy in z_copies:
                copy.wait()
            inside, _ = scan_pieces(zr, z)
            total = inside + prefix[mine, :]
            prefix[mine, :] = total
            fs[...] = total.astype(BF16)
            f_copy.start()

        feats = feature_heads(xbuf[i], wqx[...], wf01[...], wf2[...])
        for h in range(heads):
            qf[h, i] = feats[h]
            scores = nt(kf[h, i], feats[h])
            scores = jnp.where(causal, scores, 0.0).astype(BF16)
            intra[i, h * HD : (h + 1) * HD, :] = nn(vt[i, h * HD : (h + 1) * HD, :], scores)

    f_copy.wait()
    prefix[other, :] = fr[...].astype(F32)
    prefix[...] += jnp.where(c == 1, cr[...].astype(F32), 0.0)

    def finish(i, j, dst):
        state = (prefix[...] + before[i]).astype(BF16)
        for h in range(heads):
            band = slice(h * HD, (h + 1) * HD)
            raw = intra[i, band, :] + nt(state[band, :], qf[h, i])
            mean = jnp.mean(raw * raw, axis=0, keepdims=True)
            dst[band, j * CHUNK : (j + 1) * CHUNK] = (raw * lax.rsqrt(mean + EPS)).astype(BF16)

    h_copies = [send(att.at[x ^ k], out.at[x], hsend.at[k - 1], hrecv.at[k - 1], x_peers[k - 1]) for k in (1, 2, 3)]
    for k in (1, 2, 3):
        for j in range(per):
            finish((x ^ k) * per + j, j, att.at[x ^ k])
        h_copies[k - 1].start()
    for j in range(per):
        finish(x * per + j, j, out.at[x])
    for copy in h_copies:
        copy.wait()


def attention(tokens, w_query, w_key, w_value, freq):
    total, width = tokens.shape
    chunks = total // CHUNK
    cols = w_query.shape[1]
    vmem = pl.BlockSpec(memory_space=pltpu.VMEM)
    dma = pltpu.SemaphoreType.DMA
    return pl.pallas_call(
        attention_kernel,
        name="attention",
        out_shape=jax.ShapeDtypeStruct((4, cols, total // 4), BF16),
        in_specs=[pl.BlockSpec(memory_space=pl.ANY)] + [vmem] * 4,
        out_specs=vmem,
        scratch_shapes=[
            pltpu.VMEM((chunks, CHUNK, width), BF16),
            pltpu.VMEM((width, 256), BF16),
            pltpu.VMEM((width, 256), BF16),
            pltpu.VMEM((cols, width), BF16),
            pltpu.VMEM((256, 256), BF16),
            pltpu.VMEM((128, 128), BF16),
            pltpu.VMEM((3, chunks, CHUNK, 256), BF16),
            pltpu.VMEM((3, chunks, CHUNK, 256), BF16),
            pltpu.VMEM((chunks, cols, CHUNK), BF16),
            pltpu.VMEM((chunks, cols, 256), F32),
            pltpu.VMEM((chunks, cols, CHUNK), F32),
            pltpu.VMEM((cols, 256), F32),
            pltpu.VMEM((cols, 256), F32),
            pltpu.VMEM((cols, 256), BF16),
            pltpu.VMEM((cols, 256), BF16),
            pltpu.VMEM((cols // 2, 256), BF16),
            pltpu.VMEM((4, cols // 2, 256), BF16),
            pltpu.VMEM((cols // 2, 256), BF16),
            pltpu.VMEM((4, cols // 2, 256), BF16),
            pltpu.VMEM((cols // 2, 256), BF16),
            pltpu.VMEM((cols // 2, 256), BF16),
            pltpu.VMEM((4, cols, total // 4), BF16),
            dma((chunks,)),
            dma((4,)),
            dma((3,)),
            dma((3,)),
            dma((3,)),
            dma((3,)),
            dma((3,)),
            dma((3,)),
        ],
        compiler_params=pltpu.CompilerParams(
            collective_id=0, has_side_effects=True, vmem_limit_bytes=56 << 20
        ),
    )(tokens, w_query, w_key, w_value, freq)


SLOT = 8
GROUP = 32


def experts_kernel(
    cap, tok, heads, w_out, router, pick_col, pick_row, w_in, w_down, out,
    resid, hid, gates, first, second, outgoing, arrived, inner, result, returned,
    insem, osem, asem, rsem, bsem, lsem,
):
    z, y, c, x = (lax.axis_index(a) for a in AXES)
    me = ((z * 4 + y) * 2 + c) * 4 + x
    tokens, width = hid.shape
    span = GROUP * SLOT

    in_copy = pltpu.make_async_copy(
        tok.at[pl.ds(pl.multiple_of(x * tokens, tokens), tokens), :], resid, insem.at[0]
    )
    first_copy = pltpu.make_async_copy(w_in.at[0], first, insem.at[1])
    second_copy = pltpu.make_async_copy(w_down.at[0], second, insem.at[2])
    in_copy.start()
    first_copy.start()
    second_copy.start()
    returned[...] = jnp.zeros_like(returned)

    def peer(g, j):
        return (z ^ g, y ^ (j >> 3), c ^ ((j >> 2) & 1), x ^ (j & 3))

    def flat(p):
        return ((p[0] * 4 + p[1]) * 2 + p[2]) * 4 + p[3]

    barrier = pltpu.get_barrier_semaphore()

    def greet(g, j):
        pl.semaphore_signal(barrier, inc=1, device_id=peer(g, j), device_id_type=MESH)

    for g in range(4):

        @pl.loop(1 if g == 0 else 0, GROUP)
        def _(j, g=g):
            greet(g, j)

    in_copy.wait()
    hid[...] = (resid[...].astype(F32) + tn(heads[...], w_out[...])).astype(BF16)

    def gather(zz):
        base = pl.multiple_of(zz * span, span)
        picked = pick_col[pl.ds(base, span), :] == lax.broadcasted_iota(jnp.int32, (span, tokens), 1)
        rows = nn(picked.astype(F32).astype(BF16), hid[...])
        outgoing[pl.ds(zz * GROUP, GROUP)] = rows.reshape(GROUP, SLOT, width).astype(BF16)

    def exchange(src, dst, ssem, rsem, g, there=True):
        def one(j):
            p = peer(g, j)
            pltpu.make_async_remote_copy(
                src_ref=src.at[flat(p), pl.ds(0, cap)],
                dst_ref=dst.at[me, pl.ds(0, cap)],
                send_sem=ssem.at[g],
                recv_sem=rsem.at[g],
                device_id=p,
                device_id_type=MESH,
            ).start()

        @pl.loop(1 if g == 0 else 0, GROUP)
        def _(j):
            one(j)

    def drain(src, dst, ssem, rsem, g, sent):
        n = GROUP - 1 if g == 0 else GROUP
        copy = pltpu.make_async_remote_copy(
            src_ref=src.at[pl.ds(0, n), pl.ds(0, cap)],
            dst_ref=dst.at[pl.ds(0, n), pl.ds(0, cap)],
            send_sem=ssem.at[g],
            recv_sem=rsem.at[g],
            device_id=peer(1, 0),
            device_id_type=MESH,
        )
        if sent:
            copy.wait_send()
        else:
            copy.wait_recv()

    own_out = pltpu.make_async_copy(outgoing.at[me], arrived.at[me], lsem.at[0])
    own_back = pltpu.make_async_copy(result.at[me], returned.at[me], lsem.at[1])

    pl.semaphore_wait(barrier, 127)
    for g in (1, 2, 3, 0):
        gather(z ^ g)
        if g == 0:
            own_out.start()
        exchange(outgoing, arrived, osem, asem, g)

    gate = jax.nn.sigmoid(nn(hid[...], router[...])).astype(BF16)
    experts = gate.shape[1]
    slots = experts * SLOT
    spread = (
        lax.broadcasted_iota(jnp.int32, (experts, slots), 1) // SLOT
        == lax.broadcasted_iota(jnp.int32, (experts, slots), 0)
    )
    wide = nn(gate, spread.astype(F32).astype(BF16))
    mine = lax.broadcasted_iota(jnp.int32, (tokens, slots), 0) == pick_row[...]
    gates[...] = jnp.where(mine, wide, 0.0).astype(BF16)

    first_copy.wait()
    second_copy.wait()
    own_out.wait()
    for g in (1, 2, 3, 0):
        drain(outgoing, arrived, osem, asem, g, False)
        zz = z ^ g
        group = pl.ds(pl.multiple_of(zz * GROUP, GROUP), GROUP)
        rows = arrived[group].astype(F32).reshape(span, width).astype(BF16)
        for part in range(6):
            band = slice(part * 512, (part + 1) * 512)
            inner[:, band] = jax.nn.gelu(nn(rows, first[:, band]), approximate=True).astype(BF16)
        result[group] = nn(inner[...], second[...]).reshape(GROUP, SLOT, width).astype(BF16)
        if g == 0:
            own_back.start()
        exchange(result, returned, bsem, rsem, g)

    own_back.wait()
    for g in (1, 2, 3, 0):
        drain(outgoing, arrived, osem, asem, g, True)
        drain(result, returned, bsem, rsem, g, True)
        drain(result, returned, bsem, rsem, g, False)
    back = returned[...].astype(F32).reshape(slots, width).astype(BF16)
    out[...] = (hid[...].astype(F32) + nn(gates[...], back)).astype(BF16)


def experts(tokens, heads, w_out, router, picks, w_in, w_down):
    width = tokens.shape[1]
    count, _, cap = picks.shape
    rows = heads.shape[1]
    ff = w_in.shape[2]
    padded = jnp.pad(picks.reshape(count, cap), ((0, 0), (0, SLOT - cap)), constant_values=-1)
    vmem = pl.BlockSpec(memory_space=pltpu.VMEM)
    hbm = pl.BlockSpec(memory_space=pl.ANY)
    dma = pltpu.SemaphoreType.DMA
    slots = pltpu.VMEM((count, SLOT, width), BF16)
    return pl.pallas_call(
        functools.partial(experts_kernel, cap),
        name="experts",
        out_shape=jax.ShapeDtypeStruct((rows, width), BF16),
        in_specs=[hbm, vmem, vmem, vmem, vmem, vmem, hbm, hbm],
        out_specs=vmem,
        scratch_shapes=[
            pltpu.VMEM((rows, width), BF16),
            pltpu.VMEM((rows, width), BF16),
            pltpu.VMEM((rows, count * SLOT), BF16),
            pltpu.VMEM((width, ff), BF16),
            pltpu.VMEM((ff, width), BF16),
            slots,
            slots,
            pltpu.VMEM((GROUP * SLOT, ff), BF16),
            slots,
            slots,
            dma((3,)),
            dma((4,)),
            dma((4,)),
            dma((4,)),
            dma((4,)),
            dma((2,)),
        ],
        compiler_params=pltpu.CompilerParams(
            collective_id=1, has_side_effects=True, vmem_limit_bytes=56 << 20
        ),
    )(tokens, heads, w_out, router, padded.reshape(-1, 1), padded.reshape(1, -1), w_in, w_down)


def per_device(tokens, w_query, w_key, w_value, freq, w_out, router, w_in, w_down, picks):
    heads = attention(tokens, w_query, w_key, w_value, freq)
    heads = heads.reshape(-1, heads.shape[2])
    return experts(tokens, heads, w_out, router, picks, w_in, w_down)


def solution(mesh):
    split = Mesh(mesh.devices.reshape(4, 4, 2, mesh.shape["head"]), AXES)
    seq = AXES[:3]
    in_specs = (
        P(seq, None),
        P(None, "head"),
        P(None, "head"),
        P(None, "head"),
        P(),
        P(),
        P(),
        P(AXES, None, None),
        P(AXES, None, None),
        P(None, AXES, None),
    )
    return jax.shard_map(
        per_device, mesh=split, in_specs=in_specs, out_specs=P(AXES, None), check_vma=False
    )
```

```python
import functools
import math

import jax
import jax.numpy as jnp
from jax import lax
from jax.experimental import pallas as pl
from jax.experimental.pallas import tpu as pltpu
from jax.sharding import Mesh
from jax.sharding import PartitionSpec as P

MESH = pl.DeviceIdType.MESH
AXES = ("z", "y", "c", "head")
HD = 64
CHUNK = 256
EPS = 1e-06
F32 = jnp.float32
BF16 = jnp.bfloat16

SCALE = 1.0 / math.sqrt(128.0)
ROOT = math.sqrt(2.0 * SCALE)
SIN = [ROOT * v for v in (3.141582022210377, -5.167142797933202, 2.541899038850396, -0.5546362211874226)]
COS = [
    ROOT * v
    for v in (
        0.9999999535200743,
        -4.93479286153638,
        4.0584119554710245,
        -1.3318803818997542,
        0.21969719133234294,
    )
]
ROUNDER = 12582912.0


def nt(a, b):
    return lax.dot_general(a, b, (((1,), (1,)), ((), ())), preferred_element_type=F32)


def nn(a, b):
    return lax.dot_general(a, b, (((1,), (0,)), ((), ())), preferred_element_type=F32)


def tn(a, b):
    return lax.dot_general(a, b, (((0,), (0,)), ((), ())), preferred_element_type=F32)


def waves(turns):
    r = turns - ((turns + ROUNDER) - ROUNDER)
    y = r * r
    a = r * (SIN[0] + y * (SIN[1] + y * (SIN[2] + y * SIN[3])))
    b = COS[0] + y * (COS[1] + y * (COS[2] + y * (COS[3] + y * COS[4])))
    return (SCALE - a * a).astype(BF16), (a * b).astype(BF16)


def feature_heads(x, wx, wf01, wf2):
    proj = nt(x, wx).astype(BF16)
    pair, last = proj[:, :128], proj[:, 128:]
    cos01, sin01 = waves(nn(jnp.concatenate([pair, pair], axis=1), wf01))
    cos2, sin2 = waves(nn(last, wf2))
    return (
        jnp.concatenate([cos01[:, :128], sin01[:, :128]], axis=1),
        jnp.concatenate([cos01[:, 128:], sin01[:, 128:]], axis=1),
        jnp.concatenate([cos2, sin2], axis=1),
    )


SLOT = 8
GROUP = 32
HOPS = (0, 1, 2, 1)


def message_order():
    found = []
    for core in range(2):
        for k in range(64):
            a = k & 3
            b = ((k >> 2) + a) & 3
            d = ((k >> 4) + a + b) & 3
            found.append((-(HOPS[a] + HOPS[b] + HOPS[d]), k, -core, (a, b, core, d)))
    found.sort()
    return [f[3] for f in found]


ORDER = message_order()


def flat(p):
    return ((p[0] * 4 + p[1]) * 2 + p[2]) * 4 + p[3]


def layer_kernel(
    cap, tok, wq, wk, wv, freq, w_out, router, picks, w_in, w_down, out,
    xbuf, wqx, wkx, wf01, wf2, kf, qf, vt, before, intra, run, prefix,
    cs, cr, ys, yr, zs, zr, fs, fr, att, slabs,
    wo, acc, hid, onehot, gates, first, second, outgoing, arrived, inner, result, returned,
    xsem, csem, ysend, yrecv, zsend, zrecv, hsend, hrecv, insem, osem, asem, rsem, bsem, lsem,
):
    z, y, c, x = (lax.axis_index(a) for a in AXES)
    heads = 3
    chunks = xbuf.shape[0]
    per = chunks // 4
    tokens, width = hid.shape
    slots = onehot.shape[0]
    count = slots // SLOT
    span = GROUP * SLOT

    def peer(offset):
        return (z ^ offset[0], y ^ offset[1], c ^ offset[2], x ^ offset[3])

    def fetch(i):
        return pltpu.make_async_copy(
            tok.at[pl.ds(pl.multiple_of(i * CHUNK, CHUNK), CHUNK), :], xbuf.at[i], xsem.at[i]
        )

    @pl.loop(0, chunks)
    def _(i):
        fetch(i).start()

    wo_copy = pltpu.make_async_copy(w_out, wo, insem.at[0])
    first_copy = pltpu.make_async_copy(w_in.at[0], first, insem.at[1])
    second_copy = pltpu.make_async_copy(w_down.at[0], second, insem.at[2])

    returned[...] = jnp.zeros_like(returned)
    barrier = pltpu.get_barrier_semaphore()

    @pl.loop(1, 128)
    def _(k):
        pl.semaphore_signal(
            barrier,
            inc=1,
            device_id=(z ^ (k & 3), y ^ ((k >> 2) & 3), c ^ (k >> 6), x ^ ((k >> 4) & 3)),
            device_id_type=MESH,
        )

    for src, dst in ((wq, wqx), (wk, wkx)):
        dst[:192, :] = src[...]
        dst[192:, :] = src[128:192, :]
    turns = freq[...] * (1.0 / (2.0 * math.pi))
    high = turns.astype(BF16)
    low = (turns - high.astype(F32)).astype(BF16)
    wf01[...] = jnp.zeros_like(wf01)
    wf01[0:64, 0:128] = high
    wf01[64:128, 128:256] = high
    wf01[128:192, 0:128] = low
    wf01[192:256, 128:256] = low
    wf2[0:64, :] = high
    wf2[64:128, :] = low
    run[...] = jnp.zeros_like(run)

    @pl.loop(0, chunks // STEP)
    def _(p):
        for i in [p * STEP + s for s in range(STEP)]:
            fetch(i).wait()
        for i in [p * STEP + s for s in range(STEP)]:
            xs = xbuf[i]
            vals = nt(wv[...], xs).astype(BF16)
            vt[i] = vals
            feats = feature_heads(xs, wkx[...], wf01[...], wf2[...])
            before[i] = run[...]
            for h in range(heads):
                kf[h, i] = feats[h]
                run[h * HD : (h + 1) * HD, :] += nn(vals[h * HD : (h + 1) * HD, :], feats[h])

    def send(src, dst, ssem, rsem, to):
        return pltpu.make_async_remote_copy(
            src_ref=src, dst_ref=dst, send_sem=ssem, recv_sem=rsem, device_id=to, device_id_type=MESH
        )

    core = (z, y, 1 - c, x)
    y_peers = [(z, y ^ k, c, x) for k in (1, 2, 3)]
    z_peers = [(z ^ k, y, c, x) for k in (1, 2, 3)]
    half = cs.shape[0] // 2
    mine = pl.ds(pl.multiple_of(c * half, half), half)
    other = pl.ds(pl.multiple_of((1 - c) * half, half), half)
    c_copy = send(cs, cr, csem.at[0], csem.at[1], core)
    y_copies = [send(ys, yr.at[y], ysend.at[k], yrecv.at[k], y_peers[k]) for k in range(3)]
    z_copies = [send(zs, zr.at[z], zsend.at[k], zrecv.at[k], z_peers[k]) for k in range(3)]
    f_copy = send(fs, fr, csem.at[2], csem.at[3], core)

    cs[...] = run[...].astype(BF16)
    pl.semaphore_wait(barrier, 127)
    c_copy.start()
    wo_copy.start()
    first_copy.start()
    second_copy.start()

    def scan_pieces(pieces, index):
        inside = jnp.zeros(pieces.shape[1:], F32)
        total = jnp.zeros(pieces.shape[1:], F32)
        for k in range(4):
            piece = pieces[k].astype(F32)
            inside = inside + jnp.where(k < index, piece, 0.0)
            total = total + piece
        return inside, total

    rows = lax.broadcasted_iota(jnp.int32, (CHUNK, CHUNK), 0)
    columns = lax.broadcasted_iota(jnp.int32, (CHUNK, CHUNK), 1)
    causal = rows <= columns

    @pl.loop(0, chunks // STEP)
    def _(p):
        @pl.when(p == 1)
        def _():
            c_copy.wait()
            ys[...] = (run[mine, :] + cr[mine, :].astype(F32)).astype(BF16)
            yr[y] = ys[...]
            for copy in y_copies:
                copy.start()

        @pl.when(p == Y_DONE)
        def _():
            for copy in y_copies:
                copy.wait()
            inside, total = scan_pieces(yr, y)
            prefix[mine, :] = inside
            zs[...] = total.astype(BF16)
            zr[z] = zs[...]
            for copy in z_copies:
                copy.start()

        for i in [p * STEP + s for s in range(STEP)]:
            feats = feature_heads(xbuf[i], wqx[...], wf01[...], wf2[...])
            for h in range(heads):
                qf[h, i] = feats[h]
                scores = nt(kf[h, i], feats[h])
                scores = jnp.where(causal, scores, 0.0).astype(BF16)
                intra[i, h * HD : (h + 1) * HD, :] = nn(vt[i, h * HD : (h + 1) * HD, :], scores)

    for copy in z_copies:
        copy.wait()
    inside, _ = scan_pieces(zr, z)
    total = inside + prefix[mine, :]
    prefix[mine, :] = total
    fs[...] = total.astype(BF16)
    f_copy.start()
    f_copy.wait()
    prefix[other, :] = fr[...].astype(F32)
    prefix[...] += jnp.where(c == 1, cr[...].astype(F32), 0.0)

    def finish(i, j, dst):
        state = (prefix[...] + before[i]).astype(BF16)
        for h in range(heads):
            band = slice(h * HD, (h + 1) * HD)
            raw = intra[i, band, :] + nt(state[band, :], qf[h, i])
            mean = jnp.mean(raw * raw, axis=0, keepdims=True)
            dst[band, j * CHUNK : (j + 1) * CHUNK] = (raw * lax.rsqrt(mean + EPS)).astype(BF16)

    h_copies = {}
    for j in range(per):
        for k in (2, 1, 3):
            finish((x ^ k) * per + j, j, att.at[x ^ k])
            part = (slice(None), slice(j * CHUNK, (j + 1) * CHUNK))
            h_copies[k, j] = send(
                att.at[(x ^ k, *part)],
                slabs.at[(x, *part)],
                hsend.at[(k - 1) * per + j],
                hrecv.at[(k - 1) * per + j],
                (z, y, c, x ^ k),
            )
            h_copies[k, j].start()
    for j in range(per):
        finish(x * per + j, j, slabs.at[x])

    numbers = jnp.concatenate([picks[...].reshape(cap, count), jnp.full((SLOT - cap, count), -16, jnp.int32)], axis=0)
    big = (numbers >> 4).astype(F32).astype(BF16)
    small = (numbers & 15).astype(F32).astype(BF16)
    tall = lax.broadcasted_iota(jnp.int32, (slots, count), 0) >> 3
    tall = (tall == lax.broadcasted_iota(jnp.int32, (slots, count), 1)).astype(F32).astype(BF16)
    places = nt(tall, big) * 16.0 + nt(tall, small)
    place = lax.broadcasted_iota(jnp.int32, (slots, SLOT), 0) & (SLOT - 1)
    place = place == lax.broadcasted_iota(jnp.int32, (slots, SLOT), 1)
    pick_col = jnp.sum(jnp.where(place, places, 0.0), axis=1, keepdims=True).astype(jnp.int32)
    for b in range(slots // span):
        band = slice(b * span, (b + 1) * span)
        picked = pick_col[band, :] == lax.broadcasted_iota(jnp.int32, (span, tokens), 1)
        onehot[band, :] = picked.astype(F32).astype(BF16)
    wide = lax.broadcasted_iota(jnp.int32, (count, slots), 1) >> 3
    wide = (wide == lax.broadcasted_iota(jnp.int32, (count, slots), 0)).astype(F32).astype(BF16)
    places = nn(big, wide) * 16.0 + nn(small, wide)
    place = lax.broadcasted_iota(jnp.int32, (SLOT, slots), 1) & (SLOT - 1)
    place = place == lax.broadcasted_iota(jnp.int32, (SLOT, slots), 0)
    pick_row = jnp.sum(jnp.where(place, places, 0.0), axis=0, keepdims=True).astype(jnp.int32)

    def project(k):
        band = pl.ds(pl.multiple_of((x ^ k) * 192, 192), 192)
        return tn(slabs[x ^ k], wo[band, :])

    wo_copy.wait()
    resid = jnp.concatenate([xbuf[x * per + j] for j in range(per)], axis=0)
    acc[...] = resid.astype(F32) + project(0)
    for k in (1, 3):
        for j in range(per):
            h_copies[k, j].wait()
        acc[...] += project(k)
    for j in range(per):
        h_copies[2, j].wait()
    hid[...] = (acc[...] + project(2)).astype(BF16)

    me = flat((z, y, c, x))

    def drain(src, dst, ssem, rsem, g, sent):
        n = GROUP - 1 if g == 3 else GROUP
        copy = send(
            src.at[pl.ds(0, n), pl.ds(0, cap)],
            dst.at[pl.ds(0, n), pl.ds(0, cap)],
            ssem.at[g],
            rsem.at[g],
            peer(ORDER[0]),
        )
        if sent:
            copy.wait_send()
        else:
            copy.wait_recv()

    own_out = pltpu.make_async_copy(outgoing.at[me], arrived.at[count - 1], lsem.at[0])
    own_back = pltpu.make_async_copy(result.at[count - 1], returned.at[me], lsem.at[1])

    for b in range(slots // span):
        rows = nn(onehot[b * span : (b + 1) * span, :], hid[...])
        outgoing[b * GROUP : (b + 1) * GROUP] = rows.reshape(GROUP, SLOT, width).astype(BF16)
    for i in range(count - 1):
        p = peer(ORDER[i])
        g = i // GROUP
        send(
            outgoing.at[flat(p), pl.ds(0, cap)], arrived.at[i, pl.ds(0, cap)], osem.at[g], asem.at[g], p
        ).start()
    own_out.start()

    gate = jax.nn.sigmoid(nn(hid[...], router[...])).astype(BF16)
    matched = lax.broadcasted_iota(jnp.int32, (tokens, slots), 0) == pick_row
    gates[...] = jnp.where(matched, nn(gate, wide), 0.0).astype(BF16)

    first_copy.wait()
    second_copy.wait()
    own_out.wait()
    for g in range(4):
        drain(outgoing, arrived, osem, asem, g, False)
        group = slice(g * GROUP, (g + 1) * GROUP)
        rows = arrived[group].astype(F32).reshape(span, width).astype(BF16)
        for part in range(6):
            band = slice(part * 512, (part + 1) * 512)
            inner[:, band] = jax.nn.gelu(nn(rows, first[:, band]), approximate=True).astype(BF16)
        result[group] = nn(inner[...], second[...]).reshape(GROUP, SLOT, width).astype(BF16)
        for i in range(g * GROUP, min((g + 1) * GROUP, count - 1)):
            send(
                result.at[i, pl.ds(0, cap)], returned.at[me, pl.ds(0, cap)], bsem.at[g], rsem.at[g], peer(ORDER[i])
            ).start()
    own_back.start()
    own_back.wait()
    for g in range(4):
        drain(outgoing, arrived, osem, asem, g, True)
        drain(result, returned, bsem, rsem, g, True)
        drain(result, returned, bsem, rsem, g, False)
    back = returned[...].astype(F32).reshape(slots, width).astype(BF16)
    out[...] = (hid[...].astype(F32) + nn(gates[...], back)).astype(BF16)


STEP = 2
Y_DONE = 4


def per_device(tokens, w_query, w_key, w_value, freq, w_out, router, w_in, w_down, picks):
    total, width = tokens.shape
    chunks = total // CHUNK
    cols = w_query.shape[1]
    own = total // 4
    count, _, cap = picks.shape
    ff = w_in.shape[2]
    slots = count * SLOT
    vmem = pl.BlockSpec(memory_space=pltpu.VMEM)
    hbm = pl.BlockSpec(memory_space=pl.ANY)
    dma = pltpu.SemaphoreType.DMA
    buf = pltpu.VMEM
    return pl.pallas_call(
        functools.partial(layer_kernel, cap),
        name="layer",
        out_shape=jax.ShapeDtypeStruct((own, width), BF16),
        in_specs=[hbm] + [vmem] * 4 + [hbm] + [vmem] * 2 + [hbm] * 2,
        out_specs=vmem,
        scratch_shapes=[
            buf((chunks, CHUNK, width), BF16),
            buf((256, width), BF16),
            buf((256, width), BF16),
            buf((256, 256), BF16),
            buf((128, 128), BF16),
            buf((3, chunks, CHUNK, 256), BF16),
            buf((3, chunks, CHUNK, 256), BF16),
            buf((chunks, cols, CHUNK), BF16),
            buf((chunks, cols, 256), F32),
            buf((chunks, cols, CHUNK), F32),
            buf((cols, 256), F32),
            buf((cols, 256), F32),
            buf((cols, 256), BF16),
            buf((cols, 256), BF16),
            buf((cols // 2, 256), BF16),
            buf((4, cols // 2, 256), BF16),
            buf((cols // 2, 256), BF16),
            buf((4, cols // 2, 256), BF16),
            buf((cols // 2, 256), BF16),
            buf((cols // 2, 256), BF16),
            buf((4, cols, own), BF16),
            buf((4, cols, own), BF16),
            buf((width, width), BF16),
            buf((own, width), F32),
            buf((own, width), BF16),
            buf((slots, own), BF16),
            buf((own, slots), BF16),
            buf((width, ff), BF16),
            buf((ff, width), BF16),
            buf((count, SLOT, width), BF16),
            buf((count, SLOT, width), BF16),
            buf((GROUP * SLOT, ff), BF16),
            buf((count, SLOT, width), BF16),
            buf((count, SLOT, width), BF16),
            dma((chunks,)),
            dma((4,)),
            dma((3,)),
            dma((3,)),
            dma((3,)),
            dma((3,)),
            dma((9,)),
            dma((9,)),
            dma((3,)),
            dma((4,)),
            dma((4,)),
            dma((4,)),
            dma((4,)),
            dma((2,)),
        ],
        compiler_params=pltpu.CompilerParams(
            collective_id=0, has_side_effects=True, vmem_limit_bytes=62 << 20
        ),
    )(
        tokens, w_query.T, w_key.T, w_value.T, freq, w_out, router, jnp.transpose(picks, (2, 1, 0)), w_in, w_down
    )


def solution(mesh):
    split = Mesh(mesh.devices.reshape(4, 4, 2, mesh.shape["head"]), AXES)
    seq = AXES[:3]
    in_specs = (
        P(seq, None),
        P(None, "head"),
        P(None, "head"),
        P(None, "head"),
        P(),
        P(),
        P(),
        P(AXES, None, None),
        P(AXES, None, None),
        P(None, AXES, None),
    )
    return jax.shard_map(
        per_device, mesh=split, in_specs=in_specs, out_specs=P(AXES, None), check_vma=False
    )
```

```python
import functools
import math

import jax
import jax.numpy as jnp
from jax import lax
from jax.experimental import pallas as pl
from jax.experimental.pallas import tpu as pltpu
from jax.sharding import Mesh
from jax.sharding import PartitionSpec as P

MESH = pl.DeviceIdType.MESH
AXES = ("z", "y", "c", "head")
HD = 64
CHUNK = 256
EPS = 1e-06
F32 = jnp.float32
BF16 = jnp.bfloat16

SCALE = 1.0 / math.sqrt(128.0)
ROOT = math.sqrt(2.0 * SCALE)
SIN = [ROOT * v for v in (3.141582022210377, -5.167142797933202, 2.541899038850396, -0.5546362211874226)]
COS = [
    ROOT * v
    for v in (
        0.9999999535200743,
        -4.93479286153638,
        4.0584119554710245,
        -1.3318803818997542,
        0.21969719133234294,
    )
]
ROUNDER = 12582912.0


def nt(a, b):
    return lax.dot_general(a, b, (((1,), (1,)), ((), ())), preferred_element_type=F32)


def nn(a, b):
    return lax.dot_general(a, b, (((1,), (0,)), ((), ())), preferred_element_type=F32)


def tn(a, b):
    return lax.dot_general(a, b, (((0,), (0,)), ((), ())), preferred_element_type=F32)


def waves(turns):
    r = turns - ((turns + ROUNDER) - ROUNDER)
    y = r * r
    a = r * (SIN[0] + y * (SIN[1] + y * (SIN[2] + y * SIN[3])))
    b = COS[0] + y * (COS[1] + y * (COS[2] + y * (COS[3] + y * COS[4])))
    return (SCALE - a * a).astype(BF16), (a * b).astype(BF16)


def phases(proj, wf01, wf2):
    pair, last = proj[:, :128], proj[:, 128:]
    return nn(jnp.concatenate([pair, pair], axis=1), wf01), nn(last, wf2)


def feature_heads(turns):
    cos01, sin01 = waves(turns[0])
    cos2, sin2 = waves(turns[1])
    return (
        jnp.concatenate([cos01[:, :128], sin01[:, :128]], axis=1),
        jnp.concatenate([cos01[:, 128:], sin01[:, 128:]], axis=1),
        jnp.concatenate([cos2, sin2], axis=1),
    )


SLOT = 8
GROUP = 32
HOPS = (0, 1, 2, 1)


def message_order():
    found = []
    for core in range(2):
        for k in range(64):
            a = k & 3
            b = ((k >> 2) + a) & 3
            d = ((k >> 4) + a + b) & 3
            found.append((-(HOPS[a] + HOPS[b] + HOPS[d]), k, -core, (a, b, core, d)))
    found.sort()
    return [f[3] for f in found]


ORDER = message_order()


def flat(p):
    return ((p[0] * 4 + p[1]) * 2 + p[2]) * 4 + p[3]


def layer_kernel(
    cap, tok, wq, wk, wv, freq, w_out, router, picks, w_in, w_down, out,
    xbuf, even, odd, wqx, wkx, wf01, wf2, kf, qf, vt, before, intra, run, prefix,
    cs, cr, ys, yr, zs, zr, fs, fr, att, slabs,
    wo, acc, hid, onehot, gates, first, second, outgoing, arrived, inner, result, returned,
    xsem, csem, ysend, yrecv, zsend, zrecv, hsend, hrecv, insem, osem, asem, rsem, bsem, lsem,
):
    z, y, c, x = (lax.axis_index(a) for a in AXES)
    heads = 3
    chunks = xbuf.shape[0]
    per = chunks // 4
    tokens, width = hid.shape
    slots = onehot.shape[0]
    count = slots // SLOT
    span = GROUP * SLOT

    def peer(offset):
        return (z ^ offset[0], y ^ offset[1], c ^ offset[2], x ^ offset[3])

    def fetch(i):
        return pltpu.make_async_copy(
            tok.at[pl.ds(pl.multiple_of(i * CHUNK, CHUNK), CHUNK), :], xbuf.at[i], xsem.at[i]
        )

    @pl.loop(0, chunks)
    def _(i):
        fetch(i).start()

    wo_copy = pltpu.make_async_copy(w_out, wo, insem.at[0])
    first_copy = pltpu.make_async_copy(w_in.at[0], first, insem.at[1])
    second_copy = pltpu.make_async_copy(w_down.at[0], second, insem.at[2])

    returned[...] = jnp.zeros_like(returned)
    barrier = pltpu.get_barrier_semaphore()

    @pl.loop(1, 128)
    def _(k):
        pl.semaphore_signal(
            barrier,
            inc=1,
            device_id=(z ^ (k & 3), y ^ ((k >> 2) & 3), c ^ (k >> 6), x ^ ((k >> 4) & 3)),
            device_id_type=MESH,
        )

    for src, dst in ((wq, wqx), (wk, wkx)):
        dst[:192, :] = src[...]
        dst[192:, :] = src[128:192, :]
    turns = freq[...] * (1.0 / (2.0 * math.pi))
    high = turns.astype(BF16)
    low = (turns - high.astype(F32)).astype(BF16)
    wf01[...] = jnp.zeros_like(wf01)
    wf01[0:64, 0:128] = high
    wf01[64:128, 128:256] = high
    wf01[128:192, 0:128] = low
    wf01[192:256, 128:256] = low
    wf2[0:64, :] = high
    wf2[64:128, :] = low
    run[...] = jnp.zeros_like(run)

    last_chunk = chunks - 1

    def project_key(i, ahead):
        xs = xbuf[i]
        ahead[...] = nt(xs, wkx[...]).astype(BF16)
        vt[i] = nt(wv[...], xs).astype(BF16)

    def store_key(i, turns):
        for h, feats in enumerate(feature_heads(turns)):
            kf[h, i] = feats

    def absorb_key(i):
        before[i] = run[...]
        for h in range(heads):
            band = slice(h * HD, (h + 1) * HD)
            run[band, :] += nn(vt[i, band, :], kf[h, i])

    fetch(0).wait()
    project_key(0, even)

    @pl.loop(0, chunks // 2)
    def _(p):
        fetch(2 * p + 1).wait()

        @pl.when(2 * p + 2 <= last_chunk)
        def _():
            fetch(2 * p + 2).wait()

        turns = phases(even[...], wf01[...], wf2[...])
        project_key(2 * p + 1, odd)
        store_key(2 * p, turns)
        turns = phases(odd[...], wf01[...], wf2[...])
        absorb_key(2 * p)
        project_key(jnp.minimum(2 * p + 2, last_chunk), even)
        store_key(2 * p + 1, turns)
        absorb_key(2 * p + 1)

    def send(src, dst, ssem, rsem, to):
        return pltpu.make_async_remote_copy(
            src_ref=src, dst_ref=dst, send_sem=ssem, recv_sem=rsem, device_id=to, device_id_type=MESH
        )

    core = (z, y, 1 - c, x)
    y_peers = [(z, y ^ k, c, x) for k in (1, 2, 3)]
    z_peers = [(z ^ k, y, c, x) for k in (1, 2, 3)]
    half = cs.shape[0] // 2
    mine = pl.ds(pl.multiple_of(c * half, half), half)
    other = pl.ds(pl.multiple_of((1 - c) * half, half), half)
    c_copy = send(cs, cr, csem.at[0], csem.at[1], core)
    y_copies = [send(ys, yr.at[y], ysend.at[k], yrecv.at[k], y_peers[k]) for k in range(3)]
    z_copies = [send(zs, zr.at[z], zsend.at[k], zrecv.at[k], z_peers[k]) for k in range(3)]
    f_copy = send(fs, fr, csem.at[2], csem.at[3], core)

    cs[...] = run[...].astype(BF16)
    pl.semaphore_wait(barrier, 127)
    c_copy.start()
    wo_copy.start()
    first_copy.start()
    second_copy.start()

    def scan_pieces(pieces, index):
        inside = jnp.zeros(pieces.shape[1:], F32)
        total = jnp.zeros(pieces.shape[1:], F32)
        for k in range(4):
            piece = pieces[k].astype(F32)
            inside = inside + jnp.where(k < index, piece, 0.0)
            total = total + piece
        return inside, total

    rows = lax.broadcasted_iota(jnp.int32, (CHUNK, CHUNK), 0)
    columns = lax.broadcasted_iota(jnp.int32, (CHUNK, CHUNK), 1)
    causal = rows <= columns

    def project_query(i, ahead):
        ahead[...] = nt(xbuf[i], wqx[...]).astype(BF16)

    def store_query(i, turns):
        for h, feats in enumerate(feature_heads(turns)):
            qf[h, i] = feats

    def score(i):
        for h in range(heads):
            band = slice(h * HD, (h + 1) * HD)
            scores = jnp.where(causal, nt(kf[h, i], qf[h, i]), 0.0).astype(BF16)
            intra[i, band, :] = nn(vt[i, band, :], scores)

    project_query(0, even)

    @pl.loop(0, chunks // 2)
    def _(p):
        @pl.when(p == 1)
        def _():
            c_copy.wait()
            ys[...] = (run[mine, :] + cr[mine, :].astype(F32)).astype(BF16)
            yr[y] = ys[...]
            for copy in y_copies:
                copy.start()

        @pl.when(p == Y_DONE)
        def _():
            for copy in y_copies:
                copy.wait()
            inside, total = scan_pieces(yr, y)
            prefix[mine, :] = inside
            zs[...] = total.astype(BF16)
            zr[z] = zs[...]
            for copy in z_copies:
                copy.start()

        turns = phases(even[...], wf01[...], wf2[...])
        score(jnp.maximum(2 * p - 1, 0))
        project_query(2 * p + 1, odd)
        store_query(2 * p, turns)
        turns = phases(odd[...], wf01[...], wf2[...])
        score(2 * p)
        project_query(jnp.minimum(2 * p + 2, last_chunk), even)
        store_query(2 * p + 1, turns)

    score(last_chunk)
    for copy in z_copies:
        copy.wait()
    inside, _ = scan_pieces(zr, z)
    total = inside + prefix[mine, :]
    prefix[mine, :] = total
    fs[...] = total.astype(BF16)
    f_copy.start()
    f_copy.wait()
    prefix[other, :] = fr[...].astype(F32)
    prefix[...] += jnp.where(c == 1, cr[...].astype(F32), 0.0)

    def finish(i, j, dst):
        state = (prefix[...] + before[i]).astype(BF16)
        for h in range(heads):
            band = slice(h * HD, (h + 1) * HD)
            raw = intra[i, band, :] + nt(state[band, :], qf[h, i])
            mean = jnp.mean(raw * raw, axis=0, keepdims=True)
            dst[band, j * CHUNK : (j + 1) * CHUNK] = (raw * lax.rsqrt(mean + EPS)).astype(BF16)

    h_copies = {}
    for j in range(per):
        for k in (2, 1, 3):
            finish((x ^ k) * per + j, j, att.at[x ^ k])
            part = (slice(None), slice(j * CHUNK, (j + 1) * CHUNK))
            h_copies[k, j] = send(
                att.at[(x ^ k, *part)],
                slabs.at[(x, *part)],
                hsend.at[(k - 1) * per + j],
                hrecv.at[(k - 1) * per + j],
                (z, y, c, x ^ k),
            )
            h_copies[k, j].start()
    for j in range(per):
        finish(x * per + j, j, slabs.at[x])

    numbers = jnp.concatenate([picks[...].reshape(cap, count), jnp.full((SLOT - cap, count), -16, jnp.int32)], axis=0)
    big = (numbers >> 4).astype(F32).astype(BF16)
    small = (numbers & 15).astype(F32).astype(BF16)
    tall = lax.broadcasted_iota(jnp.int32, (slots, count), 0) >> 3
    tall = (tall == lax.broadcasted_iota(jnp.int32, (slots, count), 1)).astype(F32).astype(BF16)
    places = nt(tall, big) * 16.0 + nt(tall, small)
    place = lax.broadcasted_iota(jnp.int32, (slots, SLOT), 0) & (SLOT - 1)
    place = place == lax.broadcasted_iota(jnp.int32, (slots, SLOT), 1)
    pick_col = jnp.sum(jnp.where(place, places, 0.0), axis=1, keepdims=True).astype(jnp.int32)
    for b in range(slots // span):
        band = slice(b * span, (b + 1) * span)
        picked = pick_col[band, :] == lax.broadcasted_iota(jnp.int32, (span, tokens), 1)
        onehot[band, :] = picked.astype(F32).astype(BF16)
    wide = lax.broadcasted_iota(jnp.int32, (count, slots), 1) >> 3
    wide = (wide == lax.broadcasted_iota(jnp.int32, (count, slots), 0)).astype(F32).astype(BF16)
    places = nn(big, wide) * 16.0 + nn(small, wide)
    place = lax.broadcasted_iota(jnp.int32, (SLOT, slots), 1) & (SLOT - 1)
    place = place == lax.broadcasted_iota(jnp.int32, (SLOT, slots), 0)
    pick_row = jnp.sum(jnp.where(place, places, 0.0), axis=0, keepdims=True).astype(jnp.int32)

    def project(k):
        band = pl.ds(pl.multiple_of((x ^ k) * 192, 192), 192)
        return tn(slabs[x ^ k], wo[band, :])

    wo_copy.wait()
    resid = jnp.concatenate([xbuf[x * per + j] for j in range(per)], axis=0)
    acc[...] = resid.astype(F32) + project(0)
    for k in (1, 3):
        for j in range(per):
            h_copies[k, j].wait()
        acc[...] += project(k)
    for j in range(per):
        h_copies[2, j].wait()
    hid[...] = (acc[...] + project(2)).astype(BF16)

    me = flat((z, y, c, x))

    def drain(src, dst, ssem, rsem, g, sent):
        n = GROUP - 1 if g == 3 else GROUP
        copy = send(
            src.at[pl.ds(0, n), pl.ds(0, cap)],
            dst.at[pl.ds(0, n), pl.ds(0, cap)],
            ssem.at[g],
            rsem.at[g],
            peer(ORDER[0]),
        )
        if sent:
            copy.wait_send()
        else:
            copy.wait_recv()

    own_out = pltpu.make_async_copy(outgoing.at[me], arrived.at[count - 1], lsem.at[0])
    own_back = pltpu.make_async_copy(result.at[count - 1], returned.at[me], lsem.at[1])

    for b in range(slots // span):
        rows = nn(onehot[b * span : (b + 1) * span, :], hid[...])
        outgoing[b * GROUP : (b + 1) * GROUP] = rows.reshape(GROUP, SLOT, width).astype(BF16)
    for i in range(count - 1):
        p = peer(ORDER[i])
        g = i // GROUP
        send(
            outgoing.at[flat(p), pl.ds(0, cap)], arrived.at[i, pl.ds(0, cap)], osem.at[g], asem.at[g], p
        ).start()
    own_out.start()

    gate = jax.nn.sigmoid(nn(hid[...], router[...])).astype(BF16)
    matched = lax.broadcasted_iota(jnp.int32, (tokens, slots), 0) == pick_row
    gates[...] = jnp.where(matched, nn(gate, wide), 0.0).astype(BF16)

    first_copy.wait()
    second_copy.wait()
    own_out.wait()
    for g in range(4):
        drain(outgoing, arrived, osem, asem, g, False)
        group = slice(g * GROUP, (g + 1) * GROUP)
        rows = arrived[group].astype(F32).reshape(span, width).astype(BF16)
        for part in range(6):
            band = slice(part * 512, (part + 1) * 512)
            inner[:, band] = jax.nn.gelu(nn(rows, first[:, band]), approximate=True).astype(BF16)
        result[group] = nn(inner[...], second[...]).reshape(GROUP, SLOT, width).astype(BF16)
        for i in range(g * GROUP, min((g + 1) * GROUP, count - 1)):
            send(
                result.at[i, pl.ds(0, cap)], returned.at[me, pl.ds(0, cap)], bsem.at[g], rsem.at[g], peer(ORDER[i])
            ).start()
    own_back.start()
    own_back.wait()
    for g in range(4):
        drain(outgoing, arrived, osem, asem, g, True)
        drain(result, returned, bsem, rsem, g, True)
        drain(result, returned, bsem, rsem, g, False)
    back = returned[...].astype(F32).reshape(slots, width).astype(BF16)
    out[...] = (hid[...].astype(F32) + nn(gates[...], back)).astype(BF16)


Y_DONE = 4


def per_device(tokens, w_query, w_key, w_value, freq, w_out, router, w_in, w_down, picks):
    total, width = tokens.shape
    chunks = total // CHUNK
    cols = w_query.shape[1]
    own = total // 4
    count, _, cap = picks.shape
    ff = w_in.shape[2]
    slots = count * SLOT
    vmem = pl.BlockSpec(memory_space=pltpu.VMEM)
    hbm = pl.BlockSpec(memory_space=pl.ANY)
    dma = pltpu.SemaphoreType.DMA
    buf = pltpu.VMEM
    return pl.pallas_call(
        functools.partial(layer_kernel, cap),
        name="layer",
        out_shape=jax.ShapeDtypeStruct((own, width), BF16),
        in_specs=[hbm] + [vmem] * 4 + [hbm] + [vmem] * 2 + [hbm] * 2,
        out_specs=vmem,
        scratch_shapes=[
            buf((chunks, CHUNK, width), BF16),
            buf((CHUNK, 256), BF16),
            buf((CHUNK, 256), BF16),
            buf((256, width), BF16),
            buf((256, width), BF16),
            buf((256, 256), BF16),
            buf((128, 128), BF16),
            buf((3, chunks, CHUNK, 256), BF16),
            buf((3, chunks, CHUNK, 256), BF16),
            buf((chunks, cols, CHUNK), BF16),
            buf((chunks, cols, 256), F32),
            buf((chunks, cols, CHUNK), F32),
            buf((cols, 256), F32),
            buf((cols, 256), F32),
            buf((cols, 256), BF16),
            buf((cols, 256), BF16),
            buf((cols // 2, 256), BF16),
            buf((4, cols // 2, 256), BF16),
            buf((cols // 2, 256), BF16),
            buf((4, cols // 2, 256), BF16),
            buf((cols // 2, 256), BF16),
            buf((cols // 2, 256), BF16),
            buf((4, cols, own), BF16),
            buf((4, cols, own), BF16),
            buf((width, width), BF16),
            buf((own, width), F32),
            buf((own, width), BF16),
            buf((slots, own), BF16),
            buf((own, slots), BF16),
            buf((width, ff), BF16),
            buf((ff, width), BF16),
            buf((count, SLOT, width), BF16),
            buf((count, SLOT, width), BF16),
            buf((GROUP * SLOT, ff), BF16),
            buf((count, SLOT, width), BF16),
            buf((count, SLOT, width), BF16),
            dma((chunks,)),
            dma((4,)),
            dma((3,)),
            dma((3,)),
            dma((3,)),
            dma((3,)),
            dma((9,)),
            dma((9,)),
            dma((3,)),
            dma((4,)),
            dma((4,)),
            dma((4,)),
            dma((4,)),
            dma((2,)),
        ],
        compiler_params=pltpu.CompilerParams(
            collective_id=0, has_side_effects=True, vmem_limit_bytes=62 << 20
        ),
    )(
        tokens, w_query.T, w_key.T, w_value.T, freq, w_out, router, jnp.transpose(picks, (2, 1, 0)), w_in, w_down
    )


def solution(mesh):
    split = Mesh(mesh.devices.reshape(4, 4, 2, mesh.shape["head"]), AXES)
    seq = AXES[:3]
    in_specs = (
        P(seq, None),
        P(None, "head"),
        P(None, "head"),
        P(None, "head"),
        P(),
        P(),
        P(),
        P(AXES, None, None),
        P(AXES, None, None),
        P(None, AXES, None),
    )
    return jax.shard_map(
        per_device, mesh=split, in_specs=in_specs, out_specs=P(AXES, None), check_vma=False
    )
```

```python
import functools
import math

import jax
import jax.numpy as jnp
from jax import lax
from jax.experimental import pallas as pl
from jax.experimental.pallas import tpu as pltpu
from jax.sharding import Mesh
from jax.sharding import PartitionSpec as P

MESH = pl.DeviceIdType.MESH
AXES = ("z", "y", "c", "head")
HD = 64
CHUNK = 256
EPS = 1e-06
F32 = jnp.float32
BF16 = jnp.bfloat16

SCALE = 1.0 / math.sqrt(128.0)
ROOT = math.sqrt(2.0 * SCALE)
SIN = [ROOT * v for v in (3.141582022210377, -5.167142797933202, 2.541899038850396, -0.5546362211874226)]
COS = [
    ROOT * v
    for v in (
        0.9999999535200743,
        -4.93479286153638,
        4.0584119554710245,
        -1.3318803818997542,
        0.21969719133234294,
    )
]
ROUNDER = 12582912.0


def nt(a, b):
    return lax.dot_general(a, b, (((1,), (1,)), ((), ())), preferred_element_type=F32)


def nn(a, b):
    return lax.dot_general(a, b, (((1,), (0,)), ((), ())), preferred_element_type=F32)


def tn(a, b):
    return lax.dot_general(a, b, (((0,), (0,)), ((), ())), preferred_element_type=F32)


def waves(turns):
    r = turns - ((turns + ROUNDER) - ROUNDER)
    y = r * r
    a = r * (SIN[0] + y * (SIN[1] + y * (SIN[2] + y * SIN[3])))
    b = COS[0] + y * (COS[1] + y * (COS[2] + y * (COS[3] + y * COS[4])))
    return (SCALE - a * a).astype(BF16), (a * b).astype(BF16)


def phases(proj, wf01, wf2):
    pair, last = proj[:, :128], proj[:, 128:]
    return nn(jnp.concatenate([pair, pair], axis=1), wf01), nn(last, wf2)


def feature_heads(turns):
    cos01, sin01 = waves(turns[0])
    cos2, sin2 = waves(turns[1])
    return (
        jnp.concatenate([cos01[:, :128], sin01[:, :128]], axis=1),
        jnp.concatenate([cos01[:, 128:], sin01[:, 128:]], axis=1),
        jnp.concatenate([cos2, sin2], axis=1),
    )


SLOT = 8
GROUP = 32
HOPS = (0, 1, 2, 1)


def message_order():
    found = []
    for core in range(2):
        for k in range(64):
            a = k & 3
            b = ((k >> 2) + a) & 3
            d = ((k >> 4) + a + b) & 3
            found.append((-(HOPS[a] + HOPS[b] + HOPS[d]), k, -core, (a, b, core, d)))
    found.sort()
    return [f[3] for f in found]


ORDER = message_order()
CODES = [((f[0] * 4 + f[1]) * 2 + f[2]) * 4 + f[3] for f in ORDER]


def flat(p):
    return ((p[0] * 4 + p[1]) * 2 + p[2]) * 4 + p[3]


def layer_kernel(
    cap, tok, wq, wk, wv, freq, w_out, router, picks, codes, w_in, w_down, out,
    xbuf, even, odd, wqx, wkx, wf01, wf2, kf, qf, vt, before, intra, run, prefix,
    cs, cr, ys, yr, zs, zr, fs, fr, att, slabs,
    wo, acc, hid, onehot, gates, first, second, outgoing, arrived, inner, result, returned,
    xsem, csem, ysend, yrecv, zsend, zrecv, hsend, hrecv, insem, osem, asem, rsem, bsem, lsem,
):
    z, y, c, x = (lax.axis_index(a) for a in AXES)
    heads = 3
    chunks = xbuf.shape[0]
    per = chunks // 4
    tokens, width = hid.shape
    slots = onehot.shape[0]
    count = slots // SLOT
    span = GROUP * SLOT

    def peer(offset):
        return (z ^ offset[0], y ^ offset[1], c ^ offset[2], x ^ offset[3])

    def fetch(i):
        return pltpu.make_async_copy(
            tok.at[pl.ds(pl.multiple_of(i * CHUNK, CHUNK), CHUNK), :], xbuf.at[i], xsem.at[i]
        )

    @pl.loop(0, chunks)
    def _(i):
        fetch(i).start()

    wo_copy = pltpu.make_async_copy(w_out, wo, insem.at[0])
    first_copy = pltpu.make_async_copy(w_in.at[0], first, insem.at[1])
    second_copy = pltpu.make_async_copy(w_down.at[0], second, insem.at[2])

    returned[...] = jnp.zeros_like(returned)
    barrier = pltpu.get_barrier_semaphore()

    @pl.loop(1, 128)
    def _(k):
        pl.semaphore_signal(
            barrier,
            inc=1,
            device_id=(z ^ (k & 3), y ^ ((k >> 2) & 3), c ^ (k >> 6), x ^ ((k >> 4) & 3)),
            device_id_type=MESH,
        )

    for src, dst in ((wq, wqx), (wk, wkx)):
        dst[:192, :] = src[...]
        dst[192:, :] = src[128:192, :]
    turns = freq[...] * (1.0 / (2.0 * math.pi))
    high = turns.astype(BF16)
    low = (turns - high.astype(F32)).astype(BF16)
    wf01[...] = jnp.zeros_like(wf01)
    wf01[0:64, 0:128] = high
    wf01[64:128, 128:256] = high
    wf01[128:192, 0:128] = low
    wf01[192:256, 128:256] = low
    wf2[0:64, :] = high
    wf2[64:128, :] = low
    run[...] = jnp.zeros_like(run)

    last_chunk = chunks - 1

    def project_key(i, ahead):
        xs = xbuf[i]
        ahead[...] = nt(xs, wkx[...]).astype(BF16)
        vt[i] = nt(wv[...], xs).astype(BF16)

    def store_key(i, turns):
        for h, feats in enumerate(feature_heads(turns)):
            kf[h, i] = feats

    def absorb_key(i):
        before[i] = run[...]
        for h in range(heads):
            band = slice(h * HD, (h + 1) * HD)
            run[band, :] += nn(vt[i, band, :], kf[h, i])

    fetch(0).wait()
    project_key(0, even)

    @pl.loop(0, chunks // 2)
    def _(p):
        fetch(2 * p + 1).wait()

        @pl.when(2 * p + 2 <= last_chunk)
        def _():
            fetch(2 * p + 2).wait()

        turns = phases(even[...], wf01[...], wf2[...])
        project_key(2 * p + 1, odd)
        store_key(2 * p, turns)
        turns = phases(odd[...], wf01[...], wf2[...])
        absorb_key(2 * p)
        project_key(jnp.minimum(2 * p + 2, last_chunk), even)
        store_key(2 * p + 1, turns)
        absorb_key(2 * p + 1)

    def send(src, dst, ssem, rsem, to):
        return pltpu.make_async_remote_copy(
            src_ref=src, dst_ref=dst, send_sem=ssem, recv_sem=rsem, device_id=to, device_id_type=MESH
        )

    core = (z, y, 1 - c, x)
    y_peers = [(z, y ^ k, c, x) for k in (1, 2, 3)]
    z_peers = [(z ^ k, y, c, x) for k in (1, 2, 3)]
    half = cs.shape[0] // 2
    mine = pl.ds(pl.multiple_of(c * half, half), half)
    other = pl.ds(pl.multiple_of((1 - c) * half, half), half)
    c_copy = send(cs, cr, csem.at[0], csem.at[1], core)
    y_copies = [send(ys, yr.at[y], ysend.at[k], yrecv.at[k], y_peers[k]) for k in range(3)]
    z_copies = [send(zs, zr.at[z], zsend.at[k], zrecv.at[k], z_peers[k]) for k in range(3)]
    f_copy = send(fs, fr, csem.at[2], csem.at[3], core)

    cs[...] = run[...].astype(BF16)
    pl.semaphore_wait(barrier, 127)
    c_copy.start()
    wo_copy.start()
    first_copy.start()
    second_copy.start()

    def scan_pieces(pieces, index):
        inside = jnp.zeros(pieces.shape[1:], F32)
        total = jnp.zeros(pieces.shape[1:], F32)
        for k in range(4):
            piece = pieces[k].astype(F32)
            inside = inside + jnp.where(k < index, piece, 0.0)
            total = total + piece
        return inside, total

    rows = lax.broadcasted_iota(jnp.int32, (CHUNK, CHUNK), 0)
    columns = lax.broadcasted_iota(jnp.int32, (CHUNK, CHUNK), 1)
    causal = rows <= columns

    def project_query(i, ahead):
        ahead[...] = nt(xbuf[i], wqx[...]).astype(BF16)

    def store_query(i, turns):
        for h, feats in enumerate(feature_heads(turns)):
            qf[h, i] = feats

    def score(i):
        for h in range(heads):
            band = slice(h * HD, (h + 1) * HD)
            scores = jnp.where(causal, nt(kf[h, i], qf[h, i]), 0.0).astype(BF16)
            intra[i, band, :] = nn(vt[i, band, :], scores)

    project_query(0, even)

    @pl.loop(0, chunks // 2)
    def _(p):
        @pl.when(p == 1)
        def _():
            c_copy.wait()
            ys[...] = (run[mine, :] + cr[mine, :].astype(F32)).astype(BF16)
            yr[y] = ys[...]
            for copy in y_copies:
                copy.start()

        @pl.when(p == Y_DONE)
        def _():
            for copy in y_copies:
                copy.wait()
            inside, total = scan_pieces(yr, y)
            prefix[mine, :] = inside
            zs[...] = total.astype(BF16)
            zr[z] = zs[...]
            for copy in z_copies:
                copy.start()

        turns = phases(even[...], wf01[...], wf2[...])
        score(jnp.maximum(2 * p - 1, 0))
        project_query(2 * p + 1, odd)
        store_query(2 * p, turns)
        turns = phases(odd[...], wf01[...], wf2[...])
        score(2 * p)
        project_query(jnp.minimum(2 * p + 2, last_chunk), even)
        store_query(2 * p + 1, turns)

    score(last_chunk)
    for copy in z_copies:
        copy.wait()
    inside, _ = scan_pieces(zr, z)
    total = inside + prefix[mine, :]
    prefix[mine, :] = total
    fs[...] = total.astype(BF16)
    f_copy.start()
    f_copy.wait()
    prefix[other, :] = fr[...].astype(F32)
    prefix[...] += jnp.where(c == 1, cr[...].astype(F32), 0.0)

    def finish(i, j, dst):
        state = (prefix[...] + before[i]).astype(BF16)
        for h in range(heads):
            band = slice(h * HD, (h + 1) * HD)
            raw = intra[i, band, :] + nt(state[band, :], qf[h, i])
            mean = jnp.mean(raw * raw, axis=0, keepdims=True)
            dst[band, j * CHUNK : (j + 1) * CHUNK] = (raw * lax.rsqrt(mean + EPS)).astype(BF16)

    h_copies = {}
    for j in range(per):
        for k in (2, 1, 3):
            finish((x ^ k) * per + j, j, att.at[x ^ k])
            part = (slice(None), slice(j * CHUNK, (j + 1) * CHUNK))
            h_copies[k, j] = send(
                att.at[(x ^ k, *part)],
                slabs.at[(x, *part)],
                hsend.at[(k - 1) * per + j],
                hrecv.at[(k - 1) * per + j],
                (z, y, c, x ^ k),
            )
            h_copies[k, j].start()
    for j in range(per):
        finish(x * per + j, j, slabs.at[x])

    numbers = jnp.concatenate([picks[...].reshape(cap, count), jnp.full((SLOT - cap, count), -16, jnp.int32)], axis=0)
    me = flat((z, y, c, x))
    ordered = lax.broadcasted_iota(jnp.int32, (count, count), 0) == (codes[...] ^ me)
    ordered = ordered.astype(F32).astype(BF16)
    big = nn((numbers >> 4).astype(F32).astype(BF16), ordered).astype(BF16)
    small = nn((numbers & 15).astype(F32).astype(BF16), ordered).astype(BF16)
    tall = lax.broadcasted_iota(jnp.int32, (slots, count), 0) >> 3
    tall = (tall == lax.broadcasted_iota(jnp.int32, (slots, count), 1)).astype(F32).astype(BF16)
    places = nt(tall, big) * 16.0 + nt(tall, small)
    place = lax.broadcasted_iota(jnp.int32, (slots, SLOT), 0) & (SLOT - 1)
    place = place == lax.broadcasted_iota(jnp.int32, (slots, SLOT), 1)
    pick_col = jnp.sum(jnp.where(place, places, 0.0), axis=1, keepdims=True).astype(jnp.int32)
    for b in range(slots // span):
        band = slice(b * span, (b + 1) * span)
        picked = pick_col[band, :] == lax.broadcasted_iota(jnp.int32, (span, tokens), 1)
        onehot[band, :] = picked.astype(F32).astype(BF16)
    wide = lax.broadcasted_iota(jnp.int32, (count, slots), 1) >> 3
    wide = (wide == lax.broadcasted_iota(jnp.int32, (count, slots), 0)).astype(F32).astype(BF16)
    places = nn(big, wide) * 16.0 + nn(small, wide)
    place = lax.broadcasted_iota(jnp.int32, (SLOT, slots), 1) & (SLOT - 1)
    place = place == lax.broadcasted_iota(jnp.int32, (SLOT, slots), 0)
    pick_row = jnp.sum(jnp.where(place, places, 0.0), axis=0, keepdims=True).astype(jnp.int32)

    def project(k):
        band = pl.ds(pl.multiple_of((x ^ k) * 192, 192), 192)
        return tn(slabs[x ^ k], wo[band, :])

    wo_copy.wait()
    resid = jnp.concatenate([xbuf[x * per + j] for j in range(per)], axis=0)
    acc[...] = resid.astype(F32) + project(0)
    for k in (1, 3):
        for j in range(per):
            h_copies[k, j].wait()
        acc[...] += project(k)
    for j in range(per):
        h_copies[2, j].wait()
    hid[...] = (acc[...] + project(2)).astype(BF16)

    def drain(src, dst, ssem, rsem, g, sent):
        n = GROUP - 1 if g == 3 else GROUP
        copy = send(
            src.at[pl.ds(0, n), pl.ds(0, cap)],
            dst.at[pl.ds(0, n), pl.ds(0, cap)],
            ssem.at[g],
            rsem.at[g],
            peer(ORDER[0]),
        )
        if sent:
            copy.wait_send()
        else:
            copy.wait_recv()

    own_out = pltpu.make_async_copy(outgoing.at[count - 1], arrived.at[count - 1], lsem.at[0])
    own_back = pltpu.make_async_copy(result.at[count - 1], returned.at[count - 1], lsem.at[1])

    for b in range(slots // span):
        rows = nn(onehot[b * span : (b + 1) * span, :], hid[...])
        outgoing[b * GROUP : (b + 1) * GROUP] = rows.reshape(GROUP, SLOT, width).astype(BF16)
        for i in range(b * GROUP, min((b + 1) * GROUP, count - 1)):
            send(
                outgoing.at[i, pl.ds(0, cap)], arrived.at[i, pl.ds(0, cap)], osem.at[b], asem.at[b], peer(ORDER[i])
            ).start()
    own_out.start()

    gate = jax.nn.sigmoid(nn(hid[...], router[...])).astype(BF16)
    matched = lax.broadcasted_iota(jnp.int32, (tokens, slots), 0) == pick_row
    gate = nn(gate, ordered).astype(BF16)
    gates[...] = jnp.where(matched, nn(gate, wide), 0.0).astype(BF16)

    first_copy.wait()
    second_copy.wait()
    own_out.wait()
    for g in range(4):
        drain(outgoing, arrived, osem, asem, g, False)
        group = slice(g * GROUP, (g + 1) * GROUP)
        rows = arrived[group].astype(F32).reshape(span, width).astype(BF16)
        for part in range(6):
            band = slice(part * 512, (part + 1) * 512)
            inner[:, band] = jax.nn.gelu(nn(rows, first[:, band]), approximate=True).astype(BF16)
        result[group] = nn(inner[...], second[...]).reshape(GROUP, SLOT, width).astype(BF16)
        for i in range(g * GROUP, min((g + 1) * GROUP, count - 1)):
            send(
                result.at[i, pl.ds(0, cap)], returned.at[i, pl.ds(0, cap)], bsem.at[g], rsem.at[g], peer(ORDER[i])
            ).start()
    own_back.start()
    own_back.wait()

    def combine(groups):
        for g in groups:
            drain(outgoing, arrived, osem, asem, g, True)
            drain(result, returned, bsem, rsem, g, True)
            drain(result, returned, bsem, rsem, g, False)
        first_row, end = groups[0] * GROUP, (groups[-1] + 1) * GROUP
        back = returned[first_row:end].astype(F32).reshape((end - first_row) * SLOT, width).astype(BF16)
        return nn(gates[:, first_row * SLOT : end * SLOT], back)

    acc[...] = hid[...].astype(F32) + combine((0, 1, 2))
    out[...] = (acc[...] + combine((3,))).astype(BF16)


Y_DONE = 4


def per_device(tokens, w_query, w_key, w_value, freq, w_out, router, w_in, w_down, picks):
    total, width = tokens.shape
    chunks = total // CHUNK
    cols = w_query.shape[1]
    own = total // 4
    count, _, cap = picks.shape
    ff = w_in.shape[2]
    slots = count * SLOT
    vmem = pl.BlockSpec(memory_space=pltpu.VMEM)
    hbm = pl.BlockSpec(memory_space=pl.ANY)
    dma = pltpu.SemaphoreType.DMA
    buf = pltpu.VMEM
    return pl.pallas_call(
        functools.partial(layer_kernel, cap),
        name="layer",
        out_shape=jax.ShapeDtypeStruct((own, width), BF16),
        in_specs=[hbm] + [vmem] * 4 + [hbm] + [vmem] * 3 + [hbm] * 2,
        out_specs=vmem,
        scratch_shapes=[
            buf((chunks, CHUNK, width), BF16),
            buf((CHUNK, 256), BF16),
            buf((CHUNK, 256), BF16),
            buf((256, width), BF16),
            buf((256, width), BF16),
            buf((256, 256), BF16),
            buf((128, 128), BF16),
            buf((3, chunks, CHUNK, 256), BF16),
            buf((3, chunks, CHUNK, 256), BF16),
            buf((chunks, cols, CHUNK), BF16),
            buf((chunks, cols, 256), F32),
            buf((chunks, cols, CHUNK), F32),
            buf((cols, 256), F32),
            buf((cols, 256), F32),
            buf((cols, 256), BF16),
            buf((cols, 256), BF16),
            buf((cols // 2, 256), BF16),
            buf((4, cols // 2, 256), BF16),
            buf((cols // 2, 256), BF16),
            buf((4, cols // 2, 256), BF16),
            buf((cols // 2, 256), BF16),
            buf((cols // 2, 256), BF16),
            buf((4, cols, own), BF16),
            buf((4, cols, own), BF16),
            buf((width, width), BF16),
            buf((own, width), F32),
            buf((own, width), BF16),
            buf((slots, own), BF16),
            buf((own, slots), BF16),
            buf((width, ff), BF16),
            buf((ff, width), BF16),
            buf((count, SLOT, width), BF16),
            buf((count, SLOT, width), BF16),
            buf((GROUP * SLOT, ff), BF16),
            buf((count, SLOT, width), BF16),
            buf((count, SLOT, width), BF16),
            dma((chunks,)),
            dma((4,)),
            dma((3,)),
            dma((3,)),
            dma((3,)),
            dma((3,)),
            dma((9,)),
            dma((9,)),
            dma((3,)),
            dma((4,)),
            dma((4,)),
            dma((4,)),
            dma((4,)),
            dma((2,)),
        ],
        compiler_params=pltpu.CompilerParams(
            collective_id=0, has_side_effects=True, vmem_limit_bytes=62 << 20
        ),
    )(
        tokens,
        w_query.T,
        w_key.T,
        w_value.T,
        freq,
        w_out,
        router,
        jnp.transpose(picks, (2, 1, 0)),
        jnp.asarray(CODES, jnp.int32).reshape(1, count),
        w_in,
        w_down,
    )


def solution(mesh):
    split = Mesh(mesh.devices.reshape(4, 4, 2, mesh.shape["head"]), AXES)
    seq = AXES[:3]
    in_specs = (
        P(seq, None),
        P(None, "head"),
        P(None, "head"),
        P(None, "head"),
        P(),
        P(),
        P(),
        P(AXES, None, None),
        P(AXES, None, None),
        P(None, AXES, None),
    )
    return jax.shard_map(
        per_device, mesh=split, in_specs=in_specs, out_specs=P(AXES, None), check_vma=False
    )
```

```python
import functools
import math

import jax
import jax.numpy as jnp
from jax import lax
from jax.experimental import pallas as pl
from jax.experimental.pallas import tpu as pltpu
from jax.sharding import Mesh
from jax.sharding import PartitionSpec as P

MESH = pl.DeviceIdType.MESH
AXES = ("z", "y", "c", "head")
HD = 64
CHUNK = 256
EPS = 1e-06
F32 = jnp.float32
BF16 = jnp.bfloat16

SCALE = 1.0 / math.sqrt(128.0)
ROOT = math.sqrt(2.0 * SCALE)
SIN = [ROOT * v for v in (3.141582022210377, -5.167142797933202, 2.541899038850396, -0.5546362211874226)]
COS = [
    ROOT * v
    for v in (
        0.9999999535200743,
        -4.93479286153638,
        4.0584119554710245,
        -1.3318803818997542,
        0.21969719133234294,
    )
]
ROUNDER = 12582912.0


def nt(a, b):
    return lax.dot_general(a, b, (((1,), (1,)), ((), ())), preferred_element_type=F32)


def nn(a, b):
    return lax.dot_general(a, b, (((1,), (0,)), ((), ())), preferred_element_type=F32)


def tn(a, b):
    return lax.dot_general(a, b, (((0,), (0,)), ((), ())), preferred_element_type=F32)


def waves(turns):
    r = turns - ((turns + ROUNDER) - ROUNDER)
    y = r * r
    a = r * (SIN[0] + y * (SIN[1] + y * (SIN[2] + y * SIN[3])))
    b = COS[0] + y * (COS[1] + y * (COS[2] + y * (COS[3] + y * COS[4])))
    return (SCALE - a * a).astype(BF16), (a * b).astype(BF16)


def phases(proj, wf01, wf2):
    pair, last = proj[:, :128], proj[:, 128:]
    return nn(jnp.concatenate([pair, pair], axis=1), wf01), nn(last, wf2)


def feature_heads(turns):
    cos01, sin01 = waves(turns[0])
    cos2, sin2 = waves(turns[1])
    return (
        jnp.concatenate([cos01[:, :128], sin01[:, :128]], axis=1),
        jnp.concatenate([cos01[:, 128:], sin01[:, 128:]], axis=1),
        jnp.concatenate([cos2, sin2], axis=1),
    )


SLOT = 8
GROUP = 32
HOPS = (0, 1, 2, 1)


def message_order():
    found = []
    for core in range(2):
        for k in range(64):
            a = k & 3
            b = ((k >> 2) + a) & 3
            d = ((k >> 4) + a + b) & 3
            found.append((-(HOPS[a] + HOPS[b] + HOPS[d]), k, -core, (a, b, core, d)))
    found.sort()
    return [f[3] for f in found]


ORDER = message_order()
CODES = [((f[0] * 4 + f[1]) * 2 + f[2]) * 4 + f[3] for f in ORDER]


def flat(p):
    return ((p[0] * 4 + p[1]) * 2 + p[2]) * 4 + p[3]


def layer_kernel(
    cap, tok, wq, wk, wv, freq, w_out, router, picks, codes, w_in, w_down, out,
    xbuf, even, odd, wqx, wkx, wf01, wf2, kf, qf, vt, before, intra, run, prefix,
    cs, cr, ys, yr, zs, zr, fs, fr, att, slabs,
    wo, acc, hid, onehot, gates, first, second, outgoing, arrived, inner, result, returned,
    xsem, csem, ysend, yrecv, zsend, zrecv, hsend, hrecv, insem, osem, asem, rsem, bsem, lsem,
):
    z, y, c, x = (lax.axis_index(a) for a in AXES)
    heads = 3
    chunks = xbuf.shape[0]
    per = chunks // 4
    tokens, width = hid.shape
    slots = onehot.shape[0]
    count = slots // SLOT
    span = GROUP * SLOT

    def peer(offset):
        return (z ^ offset[0], y ^ offset[1], c ^ offset[2], x ^ offset[3])

    def fetch(i):
        return pltpu.make_async_copy(
            tok.at[pl.ds(pl.multiple_of(i * CHUNK, CHUNK), CHUNK), :], xbuf.at[i], xsem.at[i]
        )

    @pl.loop(0, chunks)
    def _(i):
        fetch(i).start()

    wo_copy = pltpu.make_async_copy(w_out, wo, insem.at[0])
    first_copy = pltpu.make_async_copy(w_in.at[0], first, insem.at[1])
    second_copy = pltpu.make_async_copy(w_down.at[0], second, insem.at[2])

    returned[...] = jnp.zeros_like(returned)
    barrier = pltpu.get_barrier_semaphore()

    for offset in ORDER[:-1]:
        pl.semaphore_signal(barrier, inc=1, device_id=peer(offset), device_id_type=MESH)

    for src, dst in ((wq, wqx), (wk, wkx)):
        dst[:192, :] = src[...]
        dst[192:, :] = src[128:192, :]
    turns = freq[...] * (1.0 / (2.0 * math.pi))
    high = turns.astype(BF16)
    low = (turns - high.astype(F32)).astype(BF16)
    wf01[...] = jnp.zeros_like(wf01)
    wf01[0:64, 0:128] = high
    wf01[64:128, 128:256] = high
    wf01[128:192, 0:128] = low
    wf01[192:256, 128:256] = low
    wf2[0:64, :] = high
    wf2[64:128, :] = low
    run[...] = jnp.zeros_like(run)

    last_chunk = chunks - 1

    def project_key(i, ahead):
        xs = xbuf[i]
        ahead[...] = nt(xs, wkx[...]).astype(BF16)
        vt[i] = nt(wv[...], xs).astype(BF16)

    def store_key(i, turns):
        for h, feats in enumerate(feature_heads(turns)):
            kf[h, i] = feats

    def absorb_key(i):
        before[i] = run[...]
        for h in range(heads):
            band = slice(h * HD, (h + 1) * HD)
            run[band, :] += nn(vt[i, band, :], kf[h, i])

    fetch(0).wait()
    project_key(0, even)

    @pl.loop(0, chunks // 2)
    def _(p):
        fetch(2 * p + 1).wait()

        @pl.when(2 * p + 2 <= last_chunk)
        def _():
            fetch(2 * p + 2).wait()

        turns = phases(even[...], wf01[...], wf2[...])
        project_key(2 * p + 1, odd)
        store_key(2 * p, turns)
        turns = phases(odd[...], wf01[...], wf2[...])
        absorb_key(2 * p)
        project_key(jnp.minimum(2 * p + 2, last_chunk), even)
        store_key(2 * p + 1, turns)
        absorb_key(2 * p + 1)

    def send(src, dst, ssem, rsem, to):
        return pltpu.make_async_remote_copy(
            src_ref=src, dst_ref=dst, send_sem=ssem, recv_sem=rsem, device_id=to, device_id_type=MESH
        )

    core = (z, y, 1 - c, x)
    y_peers = [(z, y ^ k, c, x) for k in (1, 2, 3)]
    z_peers = [(z ^ k, y, c, x) for k in (1, 2, 3)]
    half = cs.shape[0] // 2
    mine = pl.ds(pl.multiple_of(c * half, half), half)
    other = pl.ds(pl.multiple_of((1 - c) * half, half), half)
    c_copy = send(cs, cr, csem.at[0], csem.at[1], core)
    y_copies = [send(ys, yr.at[y], ysend.at[k], yrecv.at[k], y_peers[k]) for k in range(3)]
    z_copies = [send(zs, zr.at[z], zsend.at[k], zrecv.at[k], z_peers[k]) for k in range(3)]
    f_copy = send(fs, fr, csem.at[2], csem.at[3], core)

    cs[...] = run[...].astype(BF16)
    pl.semaphore_wait(barrier, 127)
    c_copy.start()
    wo_copy.start()
    first_copy.start()
    second_copy.start()

    def scan_pieces(pieces, index):
        inside = jnp.zeros(pieces.shape[1:], F32)
        total = jnp.zeros(pieces.shape[1:], F32)
        for k in range(4):
            piece = pieces[k].astype(F32)
            inside = inside + jnp.where(k < index, piece, 0.0)
            total = total + piece
        return inside, total

    rows = lax.broadcasted_iota(jnp.int32, (CHUNK, CHUNK), 0)
    columns = lax.broadcasted_iota(jnp.int32, (CHUNK, CHUNK), 1)
    causal = rows <= columns

    def project_query(i, ahead):
        ahead[...] = nt(xbuf[i], wqx[...]).astype(BF16)

    def store_query(i, turns):
        for h, feats in enumerate(feature_heads(turns)):
            qf[h, i] = feats

    def score(i):
        for h in range(heads):
            band = slice(h * HD, (h + 1) * HD)
            scores = jnp.where(causal, nt(kf[h, i], qf[h, i]), 0.0).astype(BF16)
            intra[i, band, :] = nn(vt[i, band, :], scores)

    project_query(0, even)

    @pl.loop(0, chunks // 2)
    def _(p):
        @pl.when(p == 1)
        def _():
            c_copy.wait()
            ys[...] = (run[mine, :] + cr[mine, :].astype(F32)).astype(BF16)
            yr[y] = ys[...]
            for copy in y_copies:
                copy.start()

        @pl.when(p == Y_DONE)
        def _():
            for copy in y_copies:
                copy.wait()
            inside, total = scan_pieces(yr, y)
            prefix[mine, :] = inside
            zs[...] = total.astype(BF16)
            zr[z] = zs[...]
            for copy in z_copies:
                copy.start()

        turns = phases(even[...], wf01[...], wf2[...])
        score(jnp.maximum(2 * p - 1, 0))
        project_query(2 * p + 1, odd)
        store_query(2 * p, turns)
        turns = phases(odd[...], wf01[...], wf2[...])
        score(2 * p)
        project_query(jnp.minimum(2 * p + 2, last_chunk), even)
        store_query(2 * p + 1, turns)

    score(last_chunk)
    for copy in z_copies:
        copy.wait()
    inside, _ = scan_pieces(zr, z)
    total = inside + prefix[mine, :]
    prefix[mine, :] = total
    fs[...] = total.astype(BF16)
    f_copy.start()
    f_copy.wait()
    prefix[other, :] = fr[...].astype(F32)
    prefix[...] += jnp.where(c == 1, cr[...].astype(F32), 0.0)

    def finish(i, j, dst):
        state = (prefix[...] + before[i]).astype(BF16)
        for h in range(heads):
            band = slice(h * HD, (h + 1) * HD)
            raw = intra[i, band, :] + nt(state[band, :], qf[h, i])
            mean = jnp.mean(raw * raw, axis=0, keepdims=True)
            dst[band, j * CHUNK : (j + 1) * CHUNK] = (raw * lax.rsqrt(mean + EPS)).astype(BF16)

    h_copies = {}
    for j in range(per):
        for k in (2, 1, 3):
            finish((x ^ k) * per + j, j, att.at[x ^ k])
            part = (slice(None), slice(j * CHUNK, (j + 1) * CHUNK))
            h_copies[k, j] = send(
                att.at[(x ^ k, *part)],
                slabs.at[(x, *part)],
                hsend.at[(k - 1) * per + j],
                hrecv.at[(k - 1) * per + j],
                (z, y, c, x ^ k),
            )
            h_copies[k, j].start()
    for j in range(per):
        finish(x * per + j, j, slabs.at[x])

    numbers = jnp.concatenate([picks[...].reshape(cap, count), jnp.full((SLOT - cap, count), -16, jnp.int32)], axis=0)
    me = flat((z, y, c, x))
    ordered = lax.broadcasted_iota(jnp.int32, (count, count), 0) == (codes[...] ^ me)
    ordered = ordered.astype(F32).astype(BF16)
    big = nn((numbers >> 4).astype(F32).astype(BF16), ordered).astype(BF16)
    small = nn((numbers & 15).astype(F32).astype(BF16), ordered).astype(BF16)
    tall = lax.broadcasted_iota(jnp.int32, (slots, count), 0) >> 3
    tall = (tall == lax.broadcasted_iota(jnp.int32, (slots, count), 1)).astype(F32).astype(BF16)
    places = nt(tall, big) * 16.0 + nt(tall, small)
    place = lax.broadcasted_iota(jnp.int32, (slots, SLOT), 0) & (SLOT - 1)
    place = place == lax.broadcasted_iota(jnp.int32, (slots, SLOT), 1)
    pick_col = jnp.sum(jnp.where(place, places, 0.0), axis=1, keepdims=True).astype(jnp.int32)
    for b in range(slots // span):
        band = slice(b * span, (b + 1) * span)
        picked = pick_col[band, :] == lax.broadcasted_iota(jnp.int32, (span, tokens), 1)
        onehot[band, :] = picked.astype(F32).astype(BF16)
    wide = lax.broadcasted_iota(jnp.int32, (count, slots), 1) >> 3
    wide = (wide == lax.broadcasted_iota(jnp.int32, (count, slots), 0)).astype(F32).astype(BF16)
    places = nn(big, wide) * 16.0 + nn(small, wide)
    place = lax.broadcasted_iota(jnp.int32, (SLOT, slots), 1) & (SLOT - 1)
    place = place == lax.broadcasted_iota(jnp.int32, (SLOT, slots), 0)
    pick_row = jnp.sum(jnp.where(place, places, 0.0), axis=0, keepdims=True).astype(jnp.int32)

    def project(k):
        band = pl.ds(pl.multiple_of((x ^ k) * 192, 192), 192)
        return tn(slabs[x ^ k], wo[band, :])

    wo_copy.wait()
    resid = jnp.concatenate([xbuf[x * per + j] for j in range(per)], axis=0)
    acc[...] = resid.astype(F32) + project(0)
    for k in (1, 3):
        for j in range(per):
            h_copies[k, j].wait()
        acc[...] += project(k)
    for j in range(per):
        h_copies[2, j].wait()
    hid[...] = (acc[...] + project(2)).astype(BF16)

    def drain(src, dst, ssem, rsem, g, sent):
        n = GROUP - 1 if g == 3 else GROUP
        copy = send(
            src.at[pl.ds(0, n), pl.ds(0, cap)],
            dst.at[pl.ds(0, n), pl.ds(0, cap)],
            ssem.at[g],
            rsem.at[g],
            peer(ORDER[0]),
        )
        if sent:
            copy.wait_send()
        else:
            copy.wait_recv()

    own_out = pltpu.make_async_copy(outgoing.at[count - 1], arrived.at[count - 1], lsem.at[0])
    own_back = pltpu.make_async_copy(result.at[count - 1], returned.at[count - 1], lsem.at[1])

    for b in range(slots // span):
        rows = nn(onehot[b * span : (b + 1) * span, :], hid[...])
        outgoing[b * GROUP : (b + 1) * GROUP] = rows.reshape(GROUP, SLOT, width).astype(BF16)
        for i in range(b * GROUP, min((b + 1) * GROUP, count - 1)):
            send(
                outgoing.at[i, pl.ds(0, cap)], arrived.at[i, pl.ds(0, cap)], osem.at[b], asem.at[b], peer(ORDER[i])
            ).start()
    own_out.start()

    gate = jax.nn.sigmoid(nn(hid[...], router[...])).astype(BF16)
    matched = lax.broadcasted_iota(jnp.int32, (tokens, slots), 0) == pick_row
    gate = nn(gate, ordered).astype(BF16)
    gates[...] = jnp.where(matched, nn(gate, wide), 0.0).astype(BF16)

    first_copy.wait()
    second_copy.wait()
    own_out.wait()
    for g in range(4):
        drain(outgoing, arrived, osem, asem, g, False)
        group = slice(g * GROUP, (g + 1) * GROUP)
        rows = arrived[group].astype(F32).reshape(span, width).astype(BF16)
        for part in range(6):
            band = slice(part * 512, (part + 1) * 512)
            inner[:, band] = jax.nn.gelu(nn(rows, first[:, band]), approximate=True).astype(BF16)
        result[group] = nn(inner[...], second[...]).reshape(GROUP, SLOT, width).astype(BF16)
        for i in range(g * GROUP, min((g + 1) * GROUP, count - 1)):
            send(
                result.at[i, pl.ds(0, cap)], returned.at[i, pl.ds(0, cap)], bsem.at[g], rsem.at[g], peer(ORDER[i])
            ).start()
    own_back.start()
    own_back.wait()

    def combine(groups):
        for g in groups:
            drain(outgoing, arrived, osem, asem, g, True)
            drain(result, returned, bsem, rsem, g, True)
            drain(result, returned, bsem, rsem, g, False)
        first_row, end = groups[0] * GROUP, (groups[-1] + 1) * GROUP
        back = returned[first_row:end].astype(F32).reshape((end - first_row) * SLOT, width).astype(BF16)
        return nn(gates[:, first_row * SLOT : end * SLOT], back)

    acc[...] = hid[...].astype(F32) + combine((0, 1, 2))
    out[...] = (acc[...] + combine((3,))).astype(BF16)


Y_DONE = 4
PIECES = 4


def hand_over_kernel(src, dst, buf, isem, osem):
    rows = buf.shape[1]
    arrive = [pltpu.make_async_copy(src.at[i * rows : (i + 1) * rows], buf.at[i], isem.at[i]) for i in range(PIECES)]
    leave = [pltpu.make_async_copy(buf.at[i], dst.at[i * rows : (i + 1) * rows], osem.at[i]) for i in range(PIECES)]
    for copy in arrive:
        copy.start()
    for i in range(PIECES):
        arrive[i].wait()
        leave[i].start()
    for copy in leave:
        copy.wait()


def per_device(tokens, w_query, w_key, w_value, freq, w_out, router, w_in, w_down, picks):
    total, width = tokens.shape
    chunks = total // CHUNK
    cols = w_query.shape[1]
    own = total // 4
    count, _, cap = picks.shape
    ff = w_in.shape[2]
    slots = count * SLOT
    vmem = pl.BlockSpec(memory_space=pltpu.VMEM)
    hbm = pl.BlockSpec(memory_space=pl.ANY)
    dma = pltpu.SemaphoreType.DMA
    buf = pltpu.VMEM
    result = pl.pallas_call(
        functools.partial(layer_kernel, cap),
        name="layer",
        out_shape=jax.ShapeDtypeStruct((own, width), BF16),
        in_specs=[hbm] + [vmem] * 4 + [hbm] + [vmem] * 3 + [hbm] * 2,
        out_specs=vmem,
        scratch_shapes=[
            buf((chunks, CHUNK, width), BF16),
            buf((CHUNK, 256), BF16),
            buf((CHUNK, 256), BF16),
            buf((256, width), BF16),
            buf((256, width), BF16),
            buf((256, 256), BF16),
            buf((128, 128), BF16),
            buf((3, chunks, CHUNK, 256), BF16),
            buf((3, chunks, CHUNK, 256), BF16),
            buf((chunks, cols, CHUNK), BF16),
            buf((chunks, cols, 256), F32),
            buf((chunks, cols, CHUNK), F32),
            buf((cols, 256), F32),
            buf((cols, 256), F32),
            buf((cols, 256), BF16),
            buf((cols, 256), BF16),
            buf((cols // 2, 256), BF16),
            buf((4, cols // 2, 256), BF16),
            buf((cols // 2, 256), BF16),
            buf((4, cols // 2, 256), BF16),
            buf((cols // 2, 256), BF16),
            buf((cols // 2, 256), BF16),
            buf((4, cols, own), BF16),
            buf((4, cols, own), BF16),
            buf((width, width), BF16),
            buf((own, width), F32),
            buf((own, width), BF16),
            buf((slots, own), BF16),
            buf((own, slots), BF16),
            buf((width, ff), BF16),
            buf((ff, width), BF16),
            buf((count, SLOT, width), BF16),
            buf((count, SLOT, width), BF16),
            buf((GROUP * SLOT, ff), BF16),
            buf((count, SLOT, width), BF16),
            buf((count, SLOT, width), BF16),
            dma((chunks,)),
            dma((4,)),
            dma((3,)),
            dma((3,)),
            dma((3,)),
            dma((3,)),
            dma((9,)),
            dma((9,)),
            dma((3,)),
            dma((4,)),
            dma((4,)),
            dma((4,)),
            dma((4,)),
            dma((2,)),
        ],
        compiler_params=pltpu.CompilerParams(
            collective_id=0, has_side_effects=True, vmem_limit_bytes=62 << 20
        ),
    )(
        tokens,
        w_query.T,
        w_key.T,
        w_value.T,
        freq,
        w_out,
        router,
        jnp.transpose(picks, (2, 1, 0)),
        jnp.asarray(CODES, jnp.int32).reshape(1, count),
        w_in,
        w_down,
    )
    return pl.pallas_call(
        hand_over_kernel,
        name="hand_over",
        out_shape=jax.ShapeDtypeStruct(result.shape, result.dtype),
        in_specs=[hbm],
        out_specs=hbm,
        scratch_shapes=[buf((PIECES, own // PIECES, width), BF16), dma((PIECES,)), dma((PIECES,))],
    )(result)


def solution(mesh):
    split = Mesh(mesh.devices.reshape(4, 4, 2, mesh.shape["head"]), AXES)
    seq = AXES[:3]
    in_specs = (
        P(seq, None),
        P(None, "head"),
        P(None, "head"),
        P(None, "head"),
        P(),
        P(),
        P(),
        P(AXES, None, None),
        P(AXES, None, None),
        P(None, AXES, None),
    )
    return jax.shard_map(
        per_device, mesh=split, in_specs=in_specs, out_specs=P(AXES, None), check_vma=False
    )
```

```python
import functools
import math

import jax
import jax.numpy as jnp
from jax import lax
from jax.experimental import pallas as pl
from jax.experimental.pallas import tpu as pltpu
from jax.sharding import Mesh
from jax.sharding import PartitionSpec as P

MESH = pl.DeviceIdType.MESH
AXES = ("z", "y", "c", "head")
HD = 64
CHUNK = 256
EPS = 1e-06
F32 = jnp.float32
BF16 = jnp.bfloat16

SCALE = 1.0 / math.sqrt(128.0)
ROOT = math.sqrt(2.0 * SCALE)
SIN = [ROOT * v for v in (3.141582022210377, -5.167142797933202, 2.541899038850396, -0.5546362211874226)]
COS = [
    ROOT * v
    for v in (
        0.9999999535200743,
        -4.93479286153638,
        4.0584119554710245,
        -1.3318803818997542,
        0.21969719133234294,
    )
]
ROUNDER = 12582912.0


def nt(a, b):
    return lax.dot_general(a, b, (((1,), (1,)), ((), ())), preferred_element_type=F32)


def nn(a, b):
    return lax.dot_general(a, b, (((1,), (0,)), ((), ())), preferred_element_type=F32)


def tn(a, b):
    return lax.dot_general(a, b, (((0,), (0,)), ((), ())), preferred_element_type=F32)


def waves(turns):
    r = turns - ((turns + ROUNDER) - ROUNDER)
    y = r * r
    a = r * (SIN[0] + y * (SIN[1] + y * (SIN[2] + y * SIN[3])))
    b = COS[0] + y * (COS[1] + y * (COS[2] + y * (COS[3] + y * COS[4])))
    return (SCALE - a * a).astype(BF16), (a * b).astype(BF16)


def phases(proj, wf01, wf2):
    pair, last = proj[:, :128], proj[:, 128:]
    return nn(jnp.concatenate([pair, pair], axis=1), wf01), nn(last, wf2)


def feature_heads(turns):
    cos01, sin01 = waves(turns[0])
    cos2, sin2 = waves(turns[1])
    return (
        jnp.concatenate([cos01[:, :128], sin01[:, :128]], axis=1),
        jnp.concatenate([cos01[:, 128:], sin01[:, 128:]], axis=1),
        jnp.concatenate([cos2, sin2], axis=1),
    )


SLOT = 8
GROUP = 32
HOPS = (0, 1, 2, 1)
PARTS = ((0, 48), (48, 96), (96, 128))
PART_OF = [g for g, (low, high) in enumerate(PARTS) for _ in range(low, high)]


def message_order():
    found = []
    for core in range(2):
        for k in range(64):
            a = k & 3
            b = ((k >> 2) + a) & 3
            d = ((k >> 4) + a + b) & 3
            found.append((-(HOPS[a] + HOPS[b] + HOPS[d]), k, -core, (a, b, core, d)))
    found.sort()
    return [f[3] for f in found]


ORDER = message_order()
CODES = [((f[0] * 4 + f[1]) * 2 + f[2]) * 4 + f[3] for f in ORDER]


def flat(p):
    return ((p[0] * 4 + p[1]) * 2 + p[2]) * 4 + p[3]


def layer_kernel(
    cap, tok, wq, wk, wv, freq, w_out, router, picks, codes, w_in, w_down, out,
    xbuf, even, odd, wqx, wkx, wf01, wf2, kf, qf, vt, before, intra, run, prefix,
    cs, cr, ys, yr, zs, zr, fs, fr, att, slabs,
    wo, acc, hid, onehot, gates, first, second, outgoing, arrived, inner, result, returned,
    xsem, csem, ysend, yrecv, zsend, zrecv, hsend, hrecv, insem, osem, asem, rsem, bsem, lsem,
):
    z, y, c, x = (lax.axis_index(a) for a in AXES)
    heads = 3
    chunks = xbuf.shape[0]
    per = chunks // 4
    tokens, width = hid.shape
    slots = onehot.shape[0]
    count = slots // SLOT
    span = GROUP * SLOT

    def peer(offset):
        return (z ^ offset[0], y ^ offset[1], c ^ offset[2], x ^ offset[3])

    def fetch(i):
        return pltpu.make_async_copy(
            tok.at[pl.ds(pl.multiple_of(i * CHUNK, CHUNK), CHUNK), :], xbuf.at[i], xsem.at[i]
        )

    @pl.loop(0, chunks)
    def _(i):
        fetch(i).start()

    wo_copy = pltpu.make_async_copy(w_out, wo, insem.at[0])
    first_copy = pltpu.make_async_copy(w_in.at[0], first, insem.at[1])
    second_copy = pltpu.make_async_copy(w_down.at[0], second, insem.at[2])

    returned[...] = jnp.zeros_like(returned)
    barrier = pltpu.get_barrier_semaphore()

    for offset in ORDER[:-1]:
        pl.semaphore_signal(barrier, inc=1, device_id=peer(offset), device_id_type=MESH)

    for src, dst in ((wq, wqx), (wk, wkx)):
        dst[:192, :] = src[...]
        dst[192:, :] = src[128:192, :]
    turns = freq[...] * (1.0 / (2.0 * math.pi))
    high = turns.astype(BF16)
    low = (turns - high.astype(F32)).astype(BF16)
    wf01[...] = jnp.zeros_like(wf01)
    wf01[0:64, 0:128] = high
    wf01[64:128, 128:256] = high
    wf01[128:192, 0:128] = low
    wf01[192:256, 128:256] = low
    wf2[0:64, :] = high
    wf2[64:128, :] = low
    run[...] = jnp.zeros_like(run)

    last_chunk = chunks - 1

    def project_key(i, ahead):
        xs = xbuf[i]
        ahead[...] = nt(xs, wkx[...]).astype(BF16)
        vt[i] = nt(wv[...], xs).astype(BF16)

    def store_key(i, turns):
        for h, feats in enumerate(feature_heads(turns)):
            kf[h, i] = feats

    def absorb_key(i):
        before[i] = run[...]
        for h in range(heads):
            band = slice(h * HD, (h + 1) * HD)
            run[band, :] += nn(vt[i, band, :], kf[h, i])

    fetch(0).wait()
    project_key(0, even)

    @pl.loop(0, chunks // 2)
    def _(p):
        fetch(2 * p + 1).wait()

        @pl.when(2 * p + 2 <= last_chunk)
        def _():
            fetch(2 * p + 2).wait()

        turns = phases(even[...], wf01[...], wf2[...])
        project_key(2 * p + 1, odd)
        store_key(2 * p, turns)
        turns = phases(odd[...], wf01[...], wf2[...])
        absorb_key(2 * p)
        project_key(jnp.minimum(2 * p + 2, last_chunk), even)
        store_key(2 * p + 1, turns)
        absorb_key(2 * p + 1)

    def send(src, dst, ssem, rsem, to):
        return pltpu.make_async_remote_copy(
            src_ref=src, dst_ref=dst, send_sem=ssem, recv_sem=rsem, device_id=to, device_id_type=MESH
        )

    core = (z, y, 1 - c, x)
    y_peers = [(z, y ^ k, c, x) for k in (1, 2, 3)]
    z_peers = [(z ^ k, y, c, x) for k in (1, 2, 3)]
    half = cs.shape[0] // 2
    mine = pl.ds(pl.multiple_of(c * half, half), half)
    other = pl.ds(pl.multiple_of((1 - c) * half, half), half)
    c_copy = send(cs, cr, csem.at[0], csem.at[1], core)
    y_copies = [send(ys, yr.at[y], ysend.at[k], yrecv.at[k], y_peers[k]) for k in range(3)]
    z_copies = [send(zs, zr.at[z], zsend.at[k], zrecv.at[k], z_peers[k]) for k in range(3)]
    f_copy = send(fs, fr, csem.at[2], csem.at[3], core)

    cs[...] = run[...].astype(BF16)
    pl.semaphore_wait(barrier, 127)
    c_copy.start()
    wo_copy.start()
    first_copy.start()
    second_copy.start()

    def scan_pieces(pieces, index):
        inside = jnp.zeros(pieces.shape[1:], F32)
        total = jnp.zeros(pieces.shape[1:], F32)
        for k in range(4):
            piece = pieces[k].astype(F32)
            inside = inside + jnp.where(k < index, piece, 0.0)
            total = total + piece
        return inside, total

    rows = lax.broadcasted_iota(jnp.int32, (CHUNK, CHUNK), 0)
    columns = lax.broadcasted_iota(jnp.int32, (CHUNK, CHUNK), 1)
    causal = rows <= columns

    def project_query(i, ahead):
        ahead[...] = nt(xbuf[i], wqx[...]).astype(BF16)

    def store_query(i, turns):
        for h, feats in enumerate(feature_heads(turns)):
            qf[h, i] = feats

    def score(i):
        for h in range(heads):
            band = slice(h * HD, (h + 1) * HD)
            scores = jnp.where(causal, nt(kf[h, i], qf[h, i]), 0.0).astype(BF16)
            intra[i, band, :] = nn(vt[i, band, :], scores)

    project_query(0, even)

    @pl.loop(0, chunks // 2)
    def _(p):
        @pl.when(p == 1)
        def _():
            c_copy.wait()
            ys[...] = (run[mine, :] + cr[mine, :].astype(F32)).astype(BF16)
            yr[y] = ys[...]
            for copy in y_copies:
                copy.start()

        @pl.when(p == Y_DONE)
        def _():
            for copy in y_copies:
                copy.wait()
            inside, total = scan_pieces(yr, y)
            prefix[mine, :] = inside
            zs[...] = total.astype(BF16)
            zr[z] = zs[...]
            for copy in z_copies:
                copy.start()

        turns = phases(even[...], wf01[...], wf2[...])
        score(jnp.maximum(2 * p - 1, 0))
        project_query(2 * p + 1, odd)
        store_query(2 * p, turns)
        turns = phases(odd[...], wf01[...], wf2[...])
        score(2 * p)
        project_query(jnp.minimum(2 * p + 2, last_chunk), even)
        store_query(2 * p + 1, turns)

    score(last_chunk)
    for copy in z_copies:
        copy.wait()
    inside, _ = scan_pieces(zr, z)
    total = inside + prefix[mine, :]
    prefix[mine, :] = total
    fs[...] = total.astype(BF16)
    f_copy.start()
    f_copy.wait()
    prefix[other, :] = fr[...].astype(F32)
    prefix[...] += jnp.where(c == 1, cr[...].astype(F32), 0.0)

    def finish(i, j, dst):
        state = (prefix[...] + before[i]).astype(BF16)
        for h in range(heads):
            band = slice(h * HD, (h + 1) * HD)
            raw = intra[i, band, :] + nt(state[band, :], qf[h, i])
            mean = jnp.mean(raw * raw, axis=0, keepdims=True)
            dst[band, j * CHUNK : (j + 1) * CHUNK] = (raw * lax.rsqrt(mean + EPS)).astype(BF16)

    h_copies = {}
    for j in range(per):
        for k in (2, 1, 3):
            finish((x ^ k) * per + j, j, att.at[x ^ k])
            part = (slice(None), slice(j * CHUNK, (j + 1) * CHUNK))
            h_copies[k, j] = send(
                att.at[(x ^ k, *part)],
                slabs.at[(x, *part)],
                hsend.at[(k - 1) * per + j],
                hrecv.at[(k - 1) * per + j],
                (z, y, c, x ^ k),
            )
            h_copies[k, j].start()
    for j in range(per):
        finish(x * per + j, j, slabs.at[x])

    numbers = jnp.concatenate([picks[...].reshape(cap, count), jnp.full((SLOT - cap, count), -16, jnp.int32)], axis=0)
    me = flat((z, y, c, x))
    ordered = lax.broadcasted_iota(jnp.int32, (count, count), 0) == (codes[...] ^ me)
    ordered = ordered.astype(F32).astype(BF16)
    big = nn((numbers >> 4).astype(F32).astype(BF16), ordered).astype(BF16)
    small = nn((numbers & 15).astype(F32).astype(BF16), ordered).astype(BF16)
    tall = lax.broadcasted_iota(jnp.int32, (slots, count), 0) >> 3
    tall = (tall == lax.broadcasted_iota(jnp.int32, (slots, count), 1)).astype(F32).astype(BF16)
    places = nt(tall, big) * 16.0 + nt(tall, small)
    place = lax.broadcasted_iota(jnp.int32, (slots, SLOT), 0) & (SLOT - 1)
    place = place == lax.broadcasted_iota(jnp.int32, (slots, SLOT), 1)
    pick_col = jnp.sum(jnp.where(place, places, 0.0), axis=1, keepdims=True).astype(jnp.int32)
    for b in range(slots // span):
        band = slice(b * span, (b + 1) * span)
        picked = pick_col[band, :] == lax.broadcasted_iota(jnp.int32, (span, tokens), 1)
        onehot[band, :] = picked.astype(F32).astype(BF16)
    wide = lax.broadcasted_iota(jnp.int32, (count, slots), 1) >> 3
    wide = (wide == lax.broadcasted_iota(jnp.int32, (count, slots), 0)).astype(F32).astype(BF16)
    places = nn(big, wide) * 16.0 + nn(small, wide)
    place = lax.broadcasted_iota(jnp.int32, (SLOT, slots), 1) & (SLOT - 1)
    place = place == lax.broadcasted_iota(jnp.int32, (SLOT, slots), 0)
    pick_row = jnp.sum(jnp.where(place, places, 0.0), axis=0, keepdims=True).astype(jnp.int32)

    def project(k):
        band = pl.ds(pl.multiple_of((x ^ k) * 192, 192), 192)
        return tn(slabs[x ^ k], wo[band, :])

    wo_copy.wait()
    resid = jnp.concatenate([xbuf[x * per + j] for j in range(per)], axis=0)
    acc[...] = resid.astype(F32) + project(0)
    for k in (1, 3):
        for j in range(per):
            h_copies[k, j].wait()
        acc[...] += project(k)
    for j in range(per):
        h_copies[2, j].wait()
    hid[...] = (acc[...] + project(2)).astype(BF16)

    def drain(src, dst, ssem, rsem, g, sent):
        n = min(PARTS[g][1], count - 1) - PARTS[g][0]
        copy = send(
            src.at[pl.ds(0, n), pl.ds(0, cap)],
            dst.at[pl.ds(0, n), pl.ds(0, cap)],
            ssem.at[g],
            rsem.at[g],
            peer(ORDER[0]),
        )
        if sent:
            copy.wait_send()
        else:
            copy.wait_recv()

    own_out = pltpu.make_async_copy(outgoing.at[count - 1], arrived.at[count - 1], lsem.at[0])
    own_back = pltpu.make_async_copy(result.at[count - 1], returned.at[count - 1], lsem.at[1])

    for b in range(slots // span):
        rows = nn(onehot[b * span : (b + 1) * span, :], hid[...])
        outgoing[b * GROUP : (b + 1) * GROUP] = rows.reshape(GROUP, SLOT, width).astype(BF16)
        for i in range(b * GROUP, min((b + 1) * GROUP, count - 1)):
            send(
                outgoing.at[i, pl.ds(0, cap)], arrived.at[i, pl.ds(0, cap)], osem.at[PART_OF[i]],
                asem.at[PART_OF[i]], peer(ORDER[i])
            ).start()
    own_out.start()

    gate = jax.nn.sigmoid(nn(hid[...], router[...])).astype(BF16)
    matched = lax.broadcasted_iota(jnp.int32, (tokens, slots), 0) == pick_row
    gate = nn(gate, ordered).astype(BF16)
    gates[...] = jnp.where(matched, nn(gate, wide), 0.0).astype(BF16)

    first_copy.wait()
    second_copy.wait()
    own_out.wait()
    for g, (low, high) in enumerate(PARTS):
        drain(outgoing, arrived, osem, asem, g, False)
        part_rows = (high - low) * SLOT
        rows = arrived[low:high].astype(F32).reshape(part_rows, width).astype(BF16)
        for part in range(6):
            band = slice(part * 512, (part + 1) * 512)
            inner[:part_rows, band] = jax.nn.gelu(nn(rows, first[:, band]), approximate=True).astype(BF16)
        result[low:high] = nn(inner[:part_rows, :], second[...]).reshape(high - low, SLOT, width).astype(BF16)
        for i in range(low, min(high, count - 1)):
            send(
                result.at[i, pl.ds(0, cap)], returned.at[i, pl.ds(0, cap)], bsem.at[g], rsem.at[g], peer(ORDER[i])
            ).start()
    own_back.start()
    own_back.wait()

    def combine(groups):
        for g in groups:
            drain(outgoing, arrived, osem, asem, g, True)
            drain(result, returned, bsem, rsem, g, True)
            drain(result, returned, bsem, rsem, g, False)
        first_row, end = PARTS[groups[0]][0], PARTS[groups[-1]][1]
        back = returned[first_row:end].astype(F32).reshape((end - first_row) * SLOT, width).astype(BF16)
        return nn(gates[:, first_row * SLOT : end * SLOT], back)

    acc[...] = hid[...].astype(F32) + combine((0, 1))
    out[...] = (acc[...] + combine((2,))).astype(BF16)


Y_DONE = 4
PIECES = 4


def hand_over_kernel(src, dst, buf, isem, osem):
    rows = buf.shape[1]
    arrive = [pltpu.make_async_copy(src.at[i * rows : (i + 1) * rows], buf.at[i], isem.at[i]) for i in range(PIECES)]
    leave = [pltpu.make_async_copy(buf.at[i], dst.at[i * rows : (i + 1) * rows], osem.at[i]) for i in range(PIECES)]
    for copy in arrive:
        copy.start()
    for i in range(PIECES):
        arrive[i].wait()
        leave[i].start()
    for copy in leave:
        copy.wait()


def per_device(tokens, w_query, w_key, w_value, freq, w_out, router, w_in, w_down, picks):
    total, width = tokens.shape
    chunks = total // CHUNK
    cols = w_query.shape[1]
    own = total // 4
    count, _, cap = picks.shape
    ff = w_in.shape[2]
    slots = count * SLOT
    vmem = pl.BlockSpec(memory_space=pltpu.VMEM)
    hbm = pl.BlockSpec(memory_space=pl.ANY)
    dma = pltpu.SemaphoreType.DMA
    buf = pltpu.VMEM
    result = pl.pallas_call(
        functools.partial(layer_kernel, cap),
        name="layer",
        out_shape=jax.ShapeDtypeStruct((own, width), BF16),
        in_specs=[hbm] + [vmem] * 4 + [hbm] + [vmem] * 3 + [hbm] * 2,
        out_specs=vmem,
        scratch_shapes=[
            buf((chunks, CHUNK, width), BF16),
            buf((CHUNK, 256), BF16),
            buf((CHUNK, 256), BF16),
            buf((256, width), BF16),
            buf((256, width), BF16),
            buf((256, 256), BF16),
            buf((128, 128), BF16),
            buf((3, chunks, CHUNK, 256), BF16),
            buf((3, chunks, CHUNK, 256), BF16),
            buf((chunks, cols, CHUNK), BF16),
            buf((chunks, cols, 256), F32),
            buf((chunks, cols, CHUNK), F32),
            buf((cols, 256), F32),
            buf((cols, 256), F32),
            buf((cols, 256), BF16),
            buf((cols, 256), BF16),
            buf((cols // 2, 256), BF16),
            buf((4, cols // 2, 256), BF16),
            buf((cols // 2, 256), BF16),
            buf((4, cols // 2, 256), BF16),
            buf((cols // 2, 256), BF16),
            buf((cols // 2, 256), BF16),
            buf((4, cols, own), BF16),
            buf((4, cols, own), BF16),
            buf((width, width), BF16),
            buf((own, width), F32),
            buf((own, width), BF16),
            buf((slots, own), BF16),
            buf((own, slots), BF16),
            buf((width, ff), BF16),
            buf((ff, width), BF16),
            buf((count, SLOT, width), BF16),
            buf((count, SLOT, width), BF16),
            buf((48 * SLOT, ff), BF16),
            buf((count, SLOT, width), BF16),
            buf((count, SLOT, width), BF16),
            dma((chunks,)),
            dma((4,)),
            dma((3,)),
            dma((3,)),
            dma((3,)),
            dma((3,)),
            dma((9,)),
            dma((9,)),
            dma((3,)),
            dma((4,)),
            dma((4,)),
            dma((4,)),
            dma((4,)),
            dma((2,)),
        ],
        compiler_params=pltpu.CompilerParams(
            collective_id=0, has_side_effects=True, vmem_limit_bytes=62 << 20
        ),
    )(
        tokens,
        w_query.T,
        w_key.T,
        w_value.T,
        freq,
        w_out,
        router,
        jnp.transpose(picks, (2, 1, 0)),
        jnp.asarray(CODES, jnp.int32).reshape(1, count),
        w_in,
        w_down,
    )
    return pl.pallas_call(
        hand_over_kernel,
        name="hand_over",
        out_shape=jax.ShapeDtypeStruct(result.shape, result.dtype),
        in_specs=[hbm],
        out_specs=hbm,
        scratch_shapes=[buf((PIECES, own // PIECES, width), BF16), dma((PIECES,)), dma((PIECES,))],
    )(result)


def solution(mesh):
    split = Mesh(mesh.devices.reshape(4, 4, 2, mesh.shape["head"]), AXES)
    seq = AXES[:3]
    in_specs = (
        P(seq, None),
        P(None, "head"),
        P(None, "head"),
        P(None, "head"),
        P(),
        P(),
        P(),
        P(AXES, None, None),
        P(AXES, None, None),
        P(None, AXES, None),
    )
    return jax.shard_map(
        per_device, mesh=split, in_specs=in_specs, out_specs=P(AXES, None), check_vma=False
    )
```
